1024 devices in a mesh: row: 64 (over y_lo, z, core), col: 16 (over y_hi, x).
Axes of the slice: x: 4, y: 8 (y_hi: 4, y_lo: 2; y = y_hi * 2 + y_lo), z: 16, core: 2. Of those that a mesh axis runs over, the one named last changes fastest.
Arguments:
- covariance: float32 [8192, 8192], P('row', 'col')
- lon_speed: float32 [8192], replicated, may hold values from 0.05 to 0.45
- lat_speed: float32 [8192], replicated, may hold values from 0.05 to 0.45
- lon_sign: int32 [8192], replicated, may hold values from 0 to 1
- lat_sign: int32 [8192], replicated, may hold values from 0 to 1
- measurement_site_position: int32 [256], replicated, may hold values from 0 to 8191, as said below
- obs_var: float32 [256], replicated, may hold values from 0.5 to 2
Outputs:
- analysis: float32 [8192, 8192], P('row', 'col')
The draws below stay inside these ranges and needn't reach their ends.
Inputs may be any that keep to these rules, and one draw needn't show every extreme that they name: `measurement_site_position`: distinct cells.
All inputs are finite; a program needn't handle non-finite values.
Results may differ from the reference program's by a relative error of at most 0.00012.
Values sent between devices are 32-bit elements; how exact they have to be, the bound alone decides.
No kernel may reach another device: no remote copies, remote signals or barrier semaphores. Data moves between devices by JAX's collectives and lax.ppermute only.
A program may use at most 32 MiB of HBM per device.

```python
import math
import jax
import jax.numpy as jnp
from jax import lax

PARALLEL_STRIPS = 64
MERIDIAN_TOTAL = 128
NOBS = 256
STEPS = 3
STATES = 8192


def draw_covariance(key, part):
    states = PARALLEL_STRIPS * MERIDIAN_TOTAL
    first, second = jax.random.split(jax.random.fold_in(key, 11))
    noise = jax.random.normal(first, (states, states), jnp.float32)
    diagonal = jnp.exp(jax.random.uniform(second, (states,), jnp.float32, 0.0, math.log(4.0)))
    spread = 1.28 / math.sqrt(states) / math.sqrt(2.0)
    return (noise + noise.T) * spread + jnp.diag(diagonal)


def draw_measurement_site_position(key, part):
    states = PARALLEL_STRIPS * MERIDIAN_TOTAL
    order = jax.random.permutation(jax.random.fold_in(key, 5), states)
    return order[:NOBS].astype(jnp.int32)


def with_ends(result, own_key, smallest, high):
    spot = [jax.random.randint(jax.random.fold_in(own_key, axis), (), 0, length) for axis, length in enumerate(result.shape)]
    widest = result.shape.index(max(result.shape))
    next_to = spot[:widest] + [(spot[widest] + 1) % result.shape[widest]] + spot[widest + 1:]
    return result.at[tuple(spot)].set(smallest).at[tuple(next_to)].set(high)


def setup_inputs(seed: int = 0) -> dict:
    key_of = jax.random.split(jax.random.key(seed), 8)
    covariance = draw_covariance(jax.random.fold_in(key_of[7], 71), 0)
    lon_speed = jnp.clip(jax.random.uniform(key_of[1], (STATES,), jnp.float32, 0.05, 0.45), 0.05, 0.45)
    lat_speed = jnp.clip(jax.random.uniform(key_of[2], (STATES,), jnp.float32, 0.05, 0.45), 0.05, 0.45)
    lon_sign = with_ends(jax.random.randint(key_of[3], (STATES,), 0, 2), jax.random.fold_in(key_of[3], 1), 0, 1).astype(jnp.int32)
    lat_sign = with_ends(jax.random.randint(key_of[4], (STATES,), 0, 2), jax.random.fold_in(key_of[4], 1), 0, 1).astype(jnp.int32)
    measurement_site_position = draw_measurement_site_position(jax.random.fold_in(key_of[7], 71), 0)
    obs_var = jnp.clip(jnp.exp(jax.random.uniform(key_of[6], (NOBS,), jnp.float32, math.log(0.5), math.log(2.0))), 0.5, 2.0)
    return {"covariance": covariance, "lon_speed": lon_speed, "lat_speed": lat_speed, "lon_sign": lon_sign, "lat_sign": lat_sign, "measurement_site_position": measurement_site_position, "obs_var": obs_var}


def advect(q, minus, plus, cu, cv, su, sv, lat_axis):
    lon_up = jnp.where(su > 0, jnp.roll(q, 1, lat_axis + 1), jnp.roll(q, -1, lat_axis + 1))
    lat_up = jnp.where(sv > 0, minus, plus)
    return q - cu * (q - lon_up) - cv * (q - lat_up)

def shifted(q, lat_axis):
    count = q.shape[lat_axis]
    zero_shape = list(q.shape)
    zero_shape[lat_axis] = 1
    zeros = jnp.zeros(zero_shape, jnp.float32)
    minus = jnp.concatenate([zeros, lax.slice_in_dim(q, 0, count - 1, axis=lat_axis)], axis=lat_axis)
    plus = jnp.concatenate([lax.slice_in_dim(q, 1, count, axis=lat_axis), zeros], axis=lat_axis)
    return (minus, plus)

def reference(covariance, lon_speed, lat_speed, lon_sign, lat_sign, measurement_site_position, obs_var):
    states = PARALLEL_STRIPS * MERIDIAN_TOTAL
    segment_breadth = min(1024, states)
    row_cu = lon_speed.reshape(PARALLEL_STRIPS, MERIDIAN_TOTAL, 1)
    row_cv = lat_speed.reshape(PARALLEL_STRIPS, MERIDIAN_TOTAL, 1)
    row_su = lon_sign.reshape(PARALLEL_STRIPS, MERIDIAN_TOTAL, 1)
    row_sv = lat_sign.reshape(PARALLEL_STRIPS, MERIDIAN_TOTAL, 1)
    segment_parts = []
    for leading_shift in range(0, states, segment_breadth):
        segment_patch = covariance[:, leading_shift:leading_shift + segment_breadth].reshape(PARALLEL_STRIPS, MERIDIAN_TOTAL, segment_breadth)
        for step in range(STEPS):
            minus, plus = shifted(segment_patch, 0)
            segment_patch = advect(segment_patch, minus, plus, row_cu, row_cv, row_su, row_sv, 0)
        segment_parts.append(segment_patch.reshape(states, segment_breadth))
    predicted_error_matrix = jnp.concatenate(segment_parts, axis=1)
    col_cu = lon_speed.reshape(1, PARALLEL_STRIPS, MERIDIAN_TOTAL)
    col_cv = lat_speed.reshape(1, PARALLEL_STRIPS, MERIDIAN_TOTAL)
    col_su = lon_sign.reshape(1, PARALLEL_STRIPS, MERIDIAN_TOTAL)
    col_sv = lat_sign.reshape(1, PARALLEL_STRIPS, MERIDIAN_TOTAL)
    segment_parts = []
    for leading_shift in range(0, states, segment_breadth):
        segment_patch = predicted_error_matrix[leading_shift:leading_shift + segment_breadth].reshape(segment_breadth, PARALLEL_STRIPS, MERIDIAN_TOTAL)
        for step in range(STEPS):
            minus, plus = shifted(segment_patch, 1)
            segment_patch = advect(segment_patch, minus, plus, col_cu, col_cv, col_su, col_sv, 1)
        segment_parts.append(segment_patch.reshape(segment_breadth, states))
    predicted_error_matrix = jnp.concatenate(segment_parts, axis=0)
    background_product_gain = predicted_error_matrix[:, measurement_site_position]
    measured_background_lines = predicted_error_matrix[measurement_site_position, :]
    hpht = measured_background_lines[:, measurement_site_position]
    innovation = hpht + jnp.diag(obs_var)
    factor = jnp.linalg.cholesky(innovation)
    weights = jax.scipy.linalg.cho_solve((factor, True), measured_background_lines)
    segment_parts = []
    for leading_shift in range(0, states, segment_breadth):
        measurement_correction = jnp.dot(background_product_gain[leading_shift:leading_shift + segment_breadth].astype(jnp.float32), weights.astype(jnp.float32), precision=lax.Precision.HIGHEST, preferred_element_type=jnp.float32)
        segment_parts.append(predicted_error_matrix[leading_shift:leading_shift + segment_breadth] - measurement_correction)
    return jnp.concatenate(segment_parts, axis=0)
```

```python
import functools

import jax
import jax.numpy as jnp
from jax import lax
from jax.experimental import pallas as pl
from jax.experimental.pallas import tpu as pltpu
from jax.sharding import Mesh
from jax.sharding import PartitionSpec as P

PARALLEL_STRIPS = 64
MERIDIAN_TOTAL = 128
STEPS = 3
HIGHEST = lax.Precision.HIGHEST
PANEL = 32
GROUP = 8
ROW = ("yl", "z", "co")
COL = ("yh", "x")


def padded_2(cells, sides, width):
    for axis, dim in sides:
        count = lax.axis_size(axis)
        ends = count - 1
        head = lax.slice_in_dim(cells, 0, width, axis=dim)
        tail = lax.slice_in_dim(cells, cells.shape[dim] - width, cells.shape[dim], axis=dim)
        cells = jnp.concatenate(
            [
                lax.ppermute(tail, axis, [(i, (i + 1) % count) for i in range(ends)]),
                cells,
                lax.ppermute(head, axis, [((i + 1) % count, i) for i in range(ends)]),
            ],
            axis=dim,
        )
    return cells


def advect(q, minus, plus, cu, cv, su, sv, lat_axis):
    lon_up = jnp.where(su > 0, jnp.roll(q, 1, lat_axis + 1), jnp.roll(q, -1, lat_axis + 1))
    lat_up = jnp.where(sv > 0, minus, plus)
    return q - cu * (q - lon_up) - cv * (q - lat_up)


def inverse_kernel(s_ref, var_ref, out_ref):
    n = s_ref.shape[0]
    s = s_ref[...]
    row_id = lax.broadcasted_iota(jnp.int32, (n, n), 0)
    col_id = lax.broadcasted_iota(jnp.int32, (n, n), 1)
    out_ref[...] = 0.5 * (s + s.T) + jnp.where(row_id == col_id, var_ref[...], 0.0)
    sub_wide = lax.broadcasted_iota(jnp.int32, (PANEL, n), 0)
    lane_wide = lax.broadcasted_iota(jnp.int32, (PANEL, n), 1)
    sub = lax.broadcasted_iota(jnp.int32, (PANEL, 128), 0)
    lane = lax.broadcasted_iota(jnp.int32, (PANEL, 128), 1)
    for at in range(0, n, PANEL):
        tile = at // 128 * 128
        rows = out_ref[at : at + PANEL, :]
        own = jnp.where(lane - (at - tile) == sub, 1.0, 0.0)
        for first in range(0, PANEL, GROUP):
            spread = [
                jnp.broadcast_to(rows[:, at + first + m : at + first + m + 1], (PANEL, 128))
                for m in range(GROUP)
            ]
            for m in range(GROUP):
                j = first + m
                factor = spread[m]
                pivot = factor[j : j + 1, :]
                inv = jnp.where(pivot > 0.0, 1.0 / pivot, jnp.nan)
                here = sub == j
                for k in range(m + 1, GROUP):
                    line = spread[k][j : j + 1, :] * inv
                    spread[k] = jnp.where(here, line, spread[k] - factor * line)
                line = own[j : j + 1, :] * inv
                own = jnp.where(here, line, own - factor * line)
                inv2 = jnp.concatenate([inv] * (n // 128), axis=1)
                factor2 = jnp.concatenate([factor] * (n // 128), axis=1)
                line = rows[j : j + 1, :] * inv2
                rows = jnp.where(sub_wide == j, line, rows - factor2 * line)
        placed = jnp.concatenate([own if t == tile else jnp.zeros_like(own) for t in range(0, n, 128)], axis=1)
        inside = (lane_wide >= at) & (lane_wide < at + PANEL)
        rows = jnp.where(inside, placed, rows)
        update = jnp.dot(out_ref[:, at : at + PANEL], rows, precision=HIGHEST, preferred_element_type=jnp.float32)
        keep = jnp.where((col_id >= at) & (col_id < at + PANEL), 0.0, out_ref[...])
        out_ref[...] = keep - update
        out_ref[at : at + PANEL, :] = rows


def spd_inverse(s, var):
    n = s.shape[0]
    return pl.pallas_call(
        inverse_kernel,
        out_shape=jax.ShapeDtypeStruct((n, n), jnp.float32),
        in_specs=[pl.BlockSpec(memory_space=pltpu.VMEM)] * 2,
        out_specs=pl.BlockSpec(memory_space=pltpu.VMEM),
        cost_estimate=pl.CostEstimate(flops=4 * n * n * n, bytes_accessed=8 * n * n, transcendentals=0),
        name="spd_inverse",
    )(s, var.reshape(1, n))


def everyone(chunk, axis):
    copies = jnp.broadcast_to(chunk, (lax.axis_size(axis), *chunk.shape))
    return lax.all_to_all(copies, axis, split_axis=0, concat_axis=0, tiled=True)


def scattered_sum(parts, axis):
    return jnp.sum(lax.all_to_all(parts, axis, split_axis=0, concat_axis=0, tiled=True), axis=0)


SWAP = [(0, 1), (1, 0)]


def halves(cells, dim, mine):
    width = cells.shape[dim] // 2
    low = lax.slice_in_dim(cells, 0, width, axis=dim)
    high = lax.slice_in_dim(cells, width, 2 * width, axis=dim)
    return jnp.where(mine == 0, low, high), jnp.where(mine == 0, high, low)


def joined(own, other, dim, mine):
    return jnp.concatenate(
        [jnp.where(mine == 0, own, other), jnp.where(mine == 0, other, own)], axis=dim
    )


def transported(covariance, lon_speed, lat_speed, lon_sign, lat_sign, row_start, col_start):
    rows_dev, cols_dev = covariance.shape
    row_bands = rows_dev // MERIDIAN_TOTAL
    col_bands = cols_dev // MERIDIAN_TOTAL

    def row_coeff(field):
        return lax.dynamic_slice_in_dim(field, row_start, rows_dev).reshape(
            row_bands, MERIDIAN_TOTAL, 1
        )

    row_cu, row_cv = (row_coeff(lon_speed), row_coeff(lat_speed))
    row_su, row_sv = (row_coeff(lon_sign), row_coeff(lat_sign))
    segment_patch = covariance
    for step in range(STEPS):
        padded = padded_2(segment_patch, ((ROW, 0),), MERIDIAN_TOTAL)
        shaped = padded.reshape(row_bands + 2, MERIDIAN_TOTAL, cols_dev)
        segment_patch = advect(
            shaped[1:-1], shaped[:-2], shaped[2:], row_cu, row_cv, row_su, row_sv, 0
        )
        segment_patch = segment_patch.reshape(rows_dev, cols_dev)
    margin = STEPS * MERIDIAN_TOTAL
    total_bands = col_bands + 2 * STEPS

    def wide_coeff(field):
        extended = jnp.pad(field, (margin, margin))
        return lax.dynamic_slice_in_dim(extended, col_start, cols_dev + 2 * margin).reshape(
            1, total_bands, MERIDIAN_TOTAL
        )

    col_cu, col_cv = (wide_coeff(lon_speed), wide_coeff(lat_speed))
    col_su, col_sv = (wide_coeff(lon_sign), wide_coeff(lat_sign))
    band_ids = col_start // MERIDIAN_TOTAL - STEPS + jnp.arange(total_bands, dtype=jnp.int32)
    inside = (
        ((band_ids >= 0) & (band_ids < PARALLEL_STRIPS))
        .astype(jnp.float32)
        .reshape(1, total_bands, 1)
    )
    padded = padded_2(segment_patch, ((COL, 1),), margin)
    current = padded.reshape(rows_dev, total_bands, MERIDIAN_TOTAL)
    offset = 0
    for step in range(STEPS):
        count = current.shape[1]
        low, high = (offset + 1, offset + count - 1)
        current = (
            advect(
                current[:, 1:-1],
                current[:, :-2],
                current[:, 2:],
                col_cu[:, low:high],
                col_cv[:, low:high],
                col_su[:, low:high],
                col_sv[:, low:high],
                1,
            )
            * inside[:, low:high]
        )
        offset = offset + 1
    return current.reshape(rows_dev, cols_dev)


def shards(
    covariance, lon_speed, lat_speed, lon_sign, lat_sign, measurement_site_position, obs_var
):
    rows_dev, cols_dev = covariance.shape
    nobs = measurement_site_position.shape[0]
    lat_half, core = lax.axis_index("yl"), lax.axis_index("co")
    row_start = lax.axis_index(ROW) * rows_dev
    col_start = lax.axis_index(COL) * cols_dev
    dot = functools.partial(
        lax.dot_general, precision=HIGHEST, preferred_element_type=jnp.float32
    )
    forecast = transported(
        covariance, lon_speed, lat_speed, lon_sign, lat_sign, row_start, col_start
    )
    site = measurement_site_position[:, None]

    def picks(start, size):
        cell = start + lax.broadcasted_iota(jnp.int32, (nobs, size), 1)
        return (cell == site).astype(jnp.float32)

    pht = dot(picks(col_start, cols_dev), forecast, (((1,), (1,)), ((), ())))
    sides = lax.axis_size(COL)
    pht = scattered_sum(pht.reshape(sides, nobs // sides, rows_dev), COL)

    half = cols_dev // 2
    own, other = halves(forecast, 1, core)
    both = joined(own, lax.ppermute(other, "co", SWAP), 0, core)
    hp = dot(picks(row_start - core * rows_dev, 2 * rows_dev), both, (((1,), (0,)), ((), ())))
    own, other = halves(hp, 0, lat_half)
    hp = own + lax.ppermute(other, "yl", SWAP)
    deep = lax.axis_size("z")
    hp = scattered_sum(hp.reshape(deep, nobs // 2 // deep, half), "z")

    hpht = dot(hp, picks(col_start + core * half, half), (((1,), (1,)), ((), ())))
    hpht = jnp.sum(everyone(hpht, COL), axis=0)
    block = jnp.concatenate([hp, hpht], axis=1)
    block = everyone(block, "z").reshape(nobs // 2, half + nobs)
    block = joined(block, lax.ppermute(block, "yl", SWAP), 0, lat_half)
    block = lax.all_gather(block, "co", axis=0)
    hp = jnp.concatenate([block[0, :, :half], block[1, :, :half]], axis=1)
    hpht = block[0, :, half:] + block[1, :, half:]

    inverse = spd_inverse(hpht, obs_var)
    pht = everyone(pht, COL).reshape(nobs, rows_dev)
    gain = dot(inverse, pht, (((1,), (0,)), ((), ())))
    return forecast - dot(gain, hp, (((0,), (0,)), ((), ())))


def solution(mesh):
    fine = Mesh(mesh.devices.reshape(2, 16, 2, 4, 4), ROW + COL)
    return jax.shard_map(
        shards,
        mesh=fine,
        in_specs=(P(ROW, COL), P(), P(), P(), P(), P(), P()),
        out_specs=P(ROW, COL),
        check_vma=False,
    )
```

```python
import functools

import jax
import jax.numpy as jnp
from jax import lax
from jax.experimental import pallas as pl
from jax.experimental.pallas import tpu as pltpu
from jax.sharding import Mesh
from jax.sharding import PartitionSpec as P

PARALLEL_STRIPS = 64
MERIDIAN_TOTAL = 128
STEPS = 3
HIGHEST = lax.Precision.HIGHEST
PANEL = 32
GROUP = 8
ROW = ("yl", "z", "co")
COL = ("yh", "x")


def padded_2(cells, sides, width):
    for axis, dim in sides:
        count = lax.axis_size(axis)
        ends = count - 1
        head = lax.slice_in_dim(cells, 0, width, axis=dim)
        tail = lax.slice_in_dim(cells, cells.shape[dim] - width, cells.shape[dim], axis=dim)
        cells = jnp.concatenate(
            [
                lax.ppermute(tail, axis, [(i, (i + 1) % count) for i in range(ends)]),
                cells,
                lax.ppermute(head, axis, [((i + 1) % count, i) for i in range(ends)]),
            ],
            axis=dim,
        )
    return cells


def advect(q, minus, plus, cu, cv, su, sv, lat_axis):
    lon_up = jnp.where(su > 0, jnp.roll(q, 1, lat_axis + 1), jnp.roll(q, -1, lat_axis + 1))
    lat_up = jnp.where(sv > 0, minus, plus)
    return q - cu * (q - lon_up) - cv * (q - lat_up)


def inverse_kernel(s_ref, var_ref, out_ref):
    n = s_ref.shape[0]
    s = s_ref[...]
    row_id = lax.broadcasted_iota(jnp.int32, (n, n), 0)
    col_id = lax.broadcasted_iota(jnp.int32, (n, n), 1)
    out_ref[...] = 0.5 * (s + s.T) + jnp.where(row_id == col_id, var_ref[...], 0.0)
    sub_wide = lax.broadcasted_iota(jnp.int32, (PANEL, n), 0)
    lane_wide = lax.broadcasted_iota(jnp.int32, (PANEL, n), 1)
    sub = lax.broadcasted_iota(jnp.int32, (PANEL, 128), 0)
    lane = lax.broadcasted_iota(jnp.int32, (PANEL, 128), 1)
    for at in range(0, n, PANEL):
        tile = at // 128 * 128
        rows = out_ref[at : at + PANEL, :]
        own = jnp.where(lane - (at - tile) == sub, 1.0, 0.0)
        for first in range(0, PANEL, GROUP):
            spread = [
                jnp.broadcast_to(rows[:, at + first + m : at + first + m + 1], (PANEL, 128))
                for m in range(GROUP)
            ]
            for m in range(GROUP):
                j = first + m
                factor = spread[m]
                pivot = factor[j : j + 1, :]
                inv = jnp.where(pivot > 0.0, 1.0 / pivot, jnp.nan)
                here = sub == j
                for k in range(m + 1, GROUP):
                    line = spread[k][j : j + 1, :] * inv
                    spread[k] = jnp.where(here, line, spread[k] - factor * line)
                line = own[j : j + 1, :] * inv
                own = jnp.where(here, line, own - factor * line)
                inv2 = jnp.concatenate([inv] * (n // 128), axis=1)
                factor2 = jnp.concatenate([factor] * (n // 128), axis=1)
                line = rows[j : j + 1, :] * inv2
                rows = jnp.where(sub_wide == j, line, rows - factor2 * line)
        placed = jnp.concatenate([own if t == tile else jnp.zeros_like(own) for t in range(0, n, 128)], axis=1)
        inside = (lane_wide >= at) & (lane_wide < at + PANEL)
        rows = jnp.where(inside, placed, rows)
        update = jnp.dot(out_ref[:, at : at + PANEL], rows, precision=HIGHEST, preferred_element_type=jnp.float32)
        keep = jnp.where((col_id >= at) & (col_id < at + PANEL), 0.0, out_ref[...])
        out_ref[...] = keep - update
        out_ref[at : at + PANEL, :] = rows


def spd_inverse(s, var):
    n = s.shape[0]
    return pl.pallas_call(
        inverse_kernel,
        out_shape=jax.ShapeDtypeStruct((n, n), jnp.float32),
        in_specs=[pl.BlockSpec(memory_space=pltpu.VMEM)] * 2,
        out_specs=pl.BlockSpec(memory_space=pltpu.VMEM),
        cost_estimate=pl.CostEstimate(flops=4 * n * n * n, bytes_accessed=8 * n * n, transcendentals=0),
        name="spd_inverse",
    )(s, var.reshape(1, n))


def everyone(chunk, axis):
    copies = jnp.broadcast_to(chunk, (lax.axis_size(axis), *chunk.shape))
    return lax.all_to_all(copies, axis, split_axis=0, concat_axis=0, tiled=True)


def scattered_sum(parts, axis):
    return jnp.sum(lax.all_to_all(parts, axis, split_axis=0, concat_axis=0, tiled=True), axis=0)


SWAP = [(0, 1), (1, 0)]


def halves(cells, dim, mine):
    width = cells.shape[dim] // 2
    low = lax.slice_in_dim(cells, 0, width, axis=dim)
    high = lax.slice_in_dim(cells, width, 2 * width, axis=dim)
    return jnp.where(mine == 0, low, high), jnp.where(mine == 0, high, low)


def joined(own, other, dim, mine):
    return jnp.concatenate(
        [jnp.where(mine == 0, own, other), jnp.where(mine == 0, other, own)], axis=dim
    )


def transported(covariance, lon_speed, lat_speed, lon_sign, lat_sign, row_start, col_start):
    rows_dev, cols_dev = covariance.shape
    row_bands = rows_dev // MERIDIAN_TOTAL
    col_bands = cols_dev // MERIDIAN_TOTAL

    def row_coeff(field):
        return lax.dynamic_slice_in_dim(field, row_start, rows_dev).reshape(
            row_bands, MERIDIAN_TOTAL, 1
        )

    row_cu, row_cv = (row_coeff(lon_speed), row_coeff(lat_speed))
    row_su, row_sv = (row_coeff(lon_sign), row_coeff(lat_sign))
    segment_patch = covariance
    for step in range(STEPS):
        padded = padded_2(segment_patch, ((ROW, 0),), MERIDIAN_TOTAL)
        shaped = padded.reshape(row_bands + 2, MERIDIAN_TOTAL, cols_dev)
        segment_patch = advect(
            shaped[1:-1], shaped[:-2], shaped[2:], row_cu, row_cv, row_su, row_sv, 0
        )
        segment_patch = segment_patch.reshape(rows_dev, cols_dev)
    margin = STEPS * MERIDIAN_TOTAL
    total_bands = col_bands + 2 * STEPS

    def wide_coeff(field):
        extended = jnp.pad(field, (margin, margin))
        return lax.dynamic_slice_in_dim(extended, col_start, cols_dev + 2 * margin).reshape(
            1, total_bands, MERIDIAN_TOTAL
        )

    col_cu, col_cv = (wide_coeff(lon_speed), wide_coeff(lat_speed))
    col_su, col_sv = (wide_coeff(lon_sign), wide_coeff(lat_sign))
    band_ids = col_start // MERIDIAN_TOTAL - STEPS + jnp.arange(total_bands, dtype=jnp.int32)
    inside = (
        ((band_ids >= 0) & (band_ids < PARALLEL_STRIPS))
        .astype(jnp.float32)
        .reshape(1, total_bands, 1)
    )
    padded = padded_2(segment_patch, ((COL, 1),), margin)
    current = padded.reshape(rows_dev, total_bands, MERIDIAN_TOTAL)
    offset = 0
    for step in range(STEPS):
        count = current.shape[1]
        low, high = (offset + 1, offset + count - 1)
        current = (
            advect(
                current[:, 1:-1],
                current[:, :-2],
                current[:, 2:],
                col_cu[:, low:high],
                col_cv[:, low:high],
                col_su[:, low:high],
                col_sv[:, low:high],
                1,
            )
            * inside[:, low:high]
        )
        offset = offset + 1
    return current.reshape(rows_dev, cols_dev)


def shards(
    covariance, lon_speed, lat_speed, lon_sign, lat_sign, measurement_site_position, obs_var
):
    rows_dev, cols_dev = covariance.shape
    nobs = measurement_site_position.shape[0]
    lat_half, core = lax.axis_index("yl"), lax.axis_index("co")
    row_start = lax.axis_index(ROW) * rows_dev
    col_start = lax.axis_index(COL) * cols_dev
    dot = functools.partial(
        lax.dot_general, precision=HIGHEST, preferred_element_type=jnp.float32
    )
    forecast = transported(
        covariance, lon_speed, lat_speed, lon_sign, lat_sign, row_start, col_start
    )
    site = measurement_site_position[:, None]

    def picks(start, size):
        cell = start + lax.broadcasted_iota(jnp.int32, (nobs, size), 1)
        return (cell == site).astype(jnp.float32)

    pht = dot(picks(col_start, cols_dev), forecast, (((1,), (1,)), ((), ())))
    sides = lax.axis_size(COL)
    pht = scattered_sum(pht.reshape(sides, nobs // sides, rows_dev), COL)

    half = cols_dev // 2
    own, other = halves(forecast, 1, core)
    both = joined(own, lax.ppermute(other, "co", SWAP), 0, core)
    hp = dot(picks(row_start - core * rows_dev, 2 * rows_dev), both, (((1,), (0,)), ((), ())))
    own, other = halves(hp, 0, lat_half)
    hp = own + lax.ppermute(other, "yl", SWAP)
    deep = lax.axis_size("z")
    hp = scattered_sum(hp.reshape(deep, nobs // 2 // deep, half), "z")

    hpht = dot(hp, picks(col_start + core * half, half), (((1,), (1,)), ((), ())))
    flat = pht.shape[1]
    mine = pht.shape[0]
    found = everyone(jnp.concatenate([pht, hpht.reshape(-1, flat)], axis=0), COL)
    pht = found[:, :mine].reshape(nobs, rows_dev)
    hpht = jnp.sum(found[:, mine:], axis=0).reshape(hpht.shape)
    block = jnp.concatenate([hp, hpht], axis=1)
    block = everyone(block, "z").reshape(nobs // 2, half + nobs)
    block = joined(block, lax.ppermute(block, "yl", SWAP), 0, lat_half)
    fellow = lax.ppermute(block, "co", SWAP)
    hp = joined(block[:, :half], fellow[:, :half], 1, core)
    hpht = block[:, half:] + fellow[:, half:]

    inverse = spd_inverse(hpht, obs_var)
    gain = dot(inverse, pht, (((1,), (0,)), ((), ())))
    return forecast - dot(gain, hp, (((0,), (0,)), ((), ())))


def solution(mesh):
    fine = Mesh(mesh.devices.reshape(2, 16, 2, 4, 4), ROW + COL)
    return jax.shard_map(
        shards,
        mesh=fine,
        in_specs=(P(ROW, COL), P(), P(), P(), P(), P(), P()),
        out_specs=P(ROW, COL),
        check_vma=False,
    )
```

```python
import functools

import jax
import jax.numpy as jnp
from jax import lax
from jax.experimental import pallas as pl
from jax.experimental.pallas import tpu as pltpu
from jax.sharding import Mesh
from jax.sharding import PartitionSpec as P

PARALLEL_STRIPS = 64
MERIDIAN_TOTAL = 128
STEPS = 3
HIGHEST = lax.Precision.HIGHEST
PANEL = 32
GROUP = 8
ROW = ("yl", "z", "co")
COL = ("yh", "x")


def padded_2(cells, sides, width):
    for axis, dim in sides:
        count = lax.axis_size(axis)
        ends = count - 1
        head = lax.slice_in_dim(cells, 0, width, axis=dim)
        tail = lax.slice_in_dim(cells, cells.shape[dim] - width, cells.shape[dim], axis=dim)
        cells = jnp.concatenate(
            [
                lax.ppermute(tail, axis, [(i, (i + 1) % count) for i in range(ends)]),
                cells,
                lax.ppermute(head, axis, [((i + 1) % count, i) for i in range(ends)]),
            ],
            axis=dim,
        )
    return cells


def advect(q, minus, plus, cu, cv, su, sv, lat_axis):
    lon_up = jnp.where(su > 0, jnp.roll(q, 1, lat_axis + 1), jnp.roll(q, -1, lat_axis + 1))
    lat_up = jnp.where(sv > 0, minus, plus)
    return q - cu * (q - lon_up) - cv * (q - lat_up)


def inverse_kernel(s_ref, var_ref, out_ref):
    n = s_ref.shape[0]
    s = s_ref[...]
    row_id = lax.broadcasted_iota(jnp.int32, (n, n), 0)
    col_id = lax.broadcasted_iota(jnp.int32, (n, n), 1)
    out_ref[...] = 0.5 * (s + s.T) + jnp.where(row_id == col_id, var_ref[...], 0.0)
    sub_wide = lax.broadcasted_iota(jnp.int32, (PANEL, n), 0)
    lane_wide = lax.broadcasted_iota(jnp.int32, (PANEL, n), 1)
    sub = lax.broadcasted_iota(jnp.int32, (PANEL, 128), 0)
    lane = lax.broadcasted_iota(jnp.int32, (PANEL, 128), 1)
    for at in range(0, n, PANEL):
        tile = at // 128 * 128
        rows = out_ref[at : at + PANEL, :]
        own = jnp.where(lane - (at - tile) == sub, 1.0, 0.0)
        for first in range(0, PANEL, GROUP):
            spread = [
                jnp.broadcast_to(rows[:, at + first + m : at + first + m + 1], (PANEL, 128))
                for m in range(GROUP)
            ]
            for m in range(GROUP):
                j = first + m
                factor = spread[m]
                pivot = factor[j : j + 1, :]
                inv = jnp.where(pivot > 0.0, 1.0 / pivot, jnp.nan)
                here = sub == j
                for k in range(m + 1, GROUP):
                    line = spread[k][j : j + 1, :] * inv
                    spread[k] = jnp.where(here, line, spread[k] - factor * line)
                line = own[j : j + 1, :] * inv
                own = jnp.where(here, line, own - factor * line)
                inv2 = jnp.concatenate([inv] * (n // 128), axis=1)
                factor2 = jnp.concatenate([factor] * (n // 128), axis=1)
                line = rows[j : j + 1, :] * inv2
                rows = jnp.where(sub_wide == j, line, rows - factor2 * line)
        placed = jnp.concatenate([own if t == tile else jnp.zeros_like(own) for t in range(0, n, 128)], axis=1)
        inside = (lane_wide >= at) & (lane_wide < at + PANEL)
        rows = jnp.where(inside, placed, rows)
        update = jnp.dot(out_ref[:, at : at + PANEL], rows, precision=HIGHEST, preferred_element_type=jnp.float32)
        keep = jnp.where((col_id >= at) & (col_id < at + PANEL), 0.0, out_ref[...])
        out_ref[...] = keep - update
        out_ref[at : at + PANEL, :] = rows


def spd_inverse(s, var):
    n = s.shape[0]
    return pl.pallas_call(
        inverse_kernel,
        out_shape=jax.ShapeDtypeStruct((n, n), jnp.float32),
        in_specs=[pl.BlockSpec(memory_space=pltpu.VMEM)] * 2,
        out_specs=pl.BlockSpec(memory_space=pltpu.VMEM),
        cost_estimate=pl.CostEstimate(flops=4 * n * n * n, bytes_accessed=8 * n * n, transcendentals=0),
        name="spd_inverse",
    )(s, var.reshape(1, n))


def footprint_kernel(start_ref, site_ref, keep_ref, west_ref, east_ref, south_ref, north_ref, cov_ref,
                     spread_ref, rows_ref, cols_ref):
    nobs = site_ref.shape[0]
    bands = keep_ref.shape[0]
    chunk = 32
    lane = lax.broadcasted_iota(jnp.int32, (chunk, MERIDIAN_TOTAL), 1)

    def footprint(first, count, store):
        total = count + 2 * STEPS

        def coeff(ref, t):
            band = first + (t - STEPS)
            inside = (band >= 0) & (band < bands)
            line = ref[pl.ds(jnp.clip(band, 0, bands - 1), 1), :]
            return jnp.where(inside, line, 0.0)

        def body(i, carry):
            at = pl.multiple_of(i * chunk, chunk)
            site = site_ref[pl.ds(at, chunk), :]
            v = [
                (site == (first + (t - STEPS)) * MERIDIAN_TOTAL + lane).astype(jnp.float32)
                for t in range(total)
            ]
            for step in range(STEPS):
                low, high = (step + 1, total - step - 1)
                new = []
                for t in range(low, high):
                    w = coeff(keep_ref, t) * v[t]
                    w = w + pltpu.roll(coeff(west_ref, t) * v[t], MERIDIAN_TOTAL - 1, 1)
                    w = w + pltpu.roll(coeff(east_ref, t) * v[t], 1, 1)
                    w = w + coeff(south_ref, t + 1) * v[t + 1]
                    w = w + coeff(north_ref, t - 1) * v[t - 1]
                    new.append(w)
                v = [None] * low + new + [None] * (total - high)
            store(at, v[STEPS : STEPS + count])
            return carry

        lax.fori_loop(0, nobs // chunk, body, 0)

    def store_rows(at, v):
        rows_ref[pl.ds(at, chunk), 0:MERIDIAN_TOTAL] = v[0]

    def store_cols(at, v):
        for b, w in enumerate(v):
            spread_ref[pl.ds(at, chunk), b * MERIDIAN_TOTAL : (b + 1) * MERIDIAN_TOTAL] = w

    footprint(start_ref[0], cov_ref.shape[0] // MERIDIAN_TOTAL, store_rows)
    footprint(start_ref[1], cov_ref.shape[1] // MERIDIAN_TOTAL, store_cols)
    cov = cov_ref[...]
    near = rows_ref[:, 0:MERIDIAN_TOTAL]
    rows_ref[...] = jnp.dot(near, cov, precision=HIGHEST, preferred_element_type=jnp.float32)
    cols_ref[...] = lax.dot_general(
        spread_ref[...], cov, (((1,), (1,)), ((), ())), precision=HIGHEST, preferred_element_type=jnp.float32
    )


def footprints(covariance, starts, site, lon_speed, lat_speed, lon_sign, lat_sign):
    rows_dev, cols_dev = covariance.shape
    nobs = site.shape[0]
    bands = lon_speed.shape[0] // MERIDIAN_TOTAL

    def grid_of(field):
        return field.reshape(bands, MERIDIAN_TOTAL)

    cu, cv = grid_of(lon_speed), grid_of(lat_speed)
    su, sv = grid_of(lon_sign) > 0, grid_of(lat_sign) > 0
    fields = [
        1.0 - cu - cv,
        jnp.where(su, cu, 0.0),
        jnp.where(su, 0.0, cu),
        jnp.where(sv, cv, 0.0),
        jnp.where(sv, 0.0, cv),
    ]
    shapes = [(nobs, cols_dev), (nobs, cols_dev), (nobs, rows_dev)]
    return pl.pallas_call(
        footprint_kernel,
        out_shape=[jax.ShapeDtypeStruct(shape, jnp.float32) for shape in shapes],
        in_specs=[pl.BlockSpec(memory_space=pltpu.SMEM)] + [pl.BlockSpec(memory_space=pltpu.VMEM)] * 7,
        out_specs=[pl.BlockSpec(memory_space=pltpu.VMEM)] * 3,
        cost_estimate=pl.CostEstimate(flops=400 * 1000 * 1000, bytes_accessed=2000000, transcendentals=0),
        name="footprints",
    )(starts, site, *fields, covariance)


def everyone(chunk, axis):
    copies = jnp.broadcast_to(chunk, (lax.axis_size(axis), *chunk.shape))
    return lax.all_to_all(copies, axis, split_axis=0, concat_axis=0, tiled=True)


def scattered_sum(parts, axis):
    return jnp.sum(lax.all_to_all(parts, axis, split_axis=0, concat_axis=0, tiled=True), axis=0)


SWAP = [(0, 1), (1, 0)]


def halves(cells, dim, mine):
    width = cells.shape[dim] // 2
    low = lax.slice_in_dim(cells, 0, width, axis=dim)
    high = lax.slice_in_dim(cells, width, 2 * width, axis=dim)
    return jnp.where(mine == 0, low, high), jnp.where(mine == 0, high, low)


def joined(own, other, dim, mine):
    return jnp.concatenate(
        [jnp.where(mine == 0, own, other), jnp.where(mine == 0, other, own)], axis=dim
    )


def row_transported(cells, lon_speed, lat_speed, lon_sign, lat_sign, row_start):
    rows_dev, width = cells.shape
    row_bands = rows_dev // MERIDIAN_TOTAL

    def row_coeff(field):
        return lax.dynamic_slice_in_dim(field, row_start, rows_dev).reshape(
            row_bands, MERIDIAN_TOTAL, 1
        )

    row_cu, row_cv = (row_coeff(lon_speed), row_coeff(lat_speed))
    row_su, row_sv = (row_coeff(lon_sign), row_coeff(lat_sign))
    for step in range(STEPS):
        padded = padded_2(cells, ((ROW, 0),), MERIDIAN_TOTAL)
        shaped = padded.reshape(row_bands + 2, MERIDIAN_TOTAL, width)
        cells = advect(
            shaped[1:-1], shaped[:-2], shaped[2:], row_cu, row_cv, row_su, row_sv, 0
        )
        cells = cells.reshape(rows_dev, width)
    return cells


def col_fields(lon_speed, lat_speed, lon_sign, lat_sign, col_start, cols_dev):
    margin = STEPS * MERIDIAN_TOTAL
    total_bands = cols_dev // MERIDIAN_TOTAL + 2 * STEPS

    def wide_coeff(field):
        extended = jnp.pad(field, (margin, margin))
        return lax.dynamic_slice_in_dim(extended, col_start, cols_dev + 2 * margin).reshape(
            1, total_bands, MERIDIAN_TOTAL
        )

    band_ids = col_start // MERIDIAN_TOTAL - STEPS + jnp.arange(total_bands, dtype=jnp.int32)
    inside = (
        ((band_ids >= 0) & (band_ids < PARALLEL_STRIPS))
        .astype(jnp.float32)
        .reshape(1, total_bands, 1)
    )
    return [wide_coeff(field) for field in (lon_speed, lat_speed, lon_sign, lat_sign)] + [inside]


def col_transported(padded, fields):
    rows, width = padded.shape
    current = padded.reshape(rows, width // MERIDIAN_TOTAL, MERIDIAN_TOTAL)
    for step in range(STEPS):
        count = current.shape[1]
        low, high = (step + 1, step + count - 1)
        cu, cv, su, sv, inside = (field[:, low:high] for field in fields)
        current = (
            advect(current[:, 1:-1], current[:, :-2], current[:, 2:], cu, cv, su, sv, 1) * inside
        )
    return current.reshape(rows, -1)


def shards(
    covariance, lon_speed, lat_speed, lon_sign, lat_sign, measurement_site_position, obs_var
):
    rows_dev, cols_dev = covariance.shape
    nobs = measurement_site_position.shape[0]
    lat_half, core = lax.axis_index("yl"), lax.axis_index("co")
    row, col = lax.axis_index(ROW), lax.axis_index(COL)
    row_start, col_start = row * rows_dev, col * cols_dev
    margin = STEPS * MERIDIAN_TOTAL
    dot = functools.partial(
        lax.dot_general, precision=HIGHEST, preferred_element_type=jnp.float32
    )
    winds = (lon_speed, lat_speed, lon_sign, lat_sign)
    site = measurement_site_position[:, None]
    starts = jnp.stack([row_start, col_start]) // MERIDIAN_TOTAL
    spread, hp, pht = footprints(covariance, starts, site, *winds)

    own, other = halves(hp, 0, core)
    fellow = lax.ppermute(other, "co", SWAP)
    sides = lax.axis_size(COL)
    pht = scattered_sum(pht.reshape(sides, nobs // sides, rows_dev), COL)
    own, other = halves(own + fellow, 0, lat_half)
    hp = own + lax.ppermute(other, "yl", SWAP)
    deep = lax.axis_size("z")
    hp = scattered_sum(hp.reshape(deep, nobs // 4 // deep, cols_dev), "z")

    forecast = row_transported(
        jnp.concatenate([covariance, pht.T], axis=1), *winds, row_start
    )
    pht = forecast[:, cols_dev:].T
    fields = col_fields(*winds, col_start, cols_dev)
    forecast = col_transported(padded_2(forecast[:, :cols_dev], ((COL, 1),), margin), fields)

    hpht = dot(hp, spread, (((1,), (1,)), ((), ())))
    found = everyone(jnp.concatenate([hp, hpht], axis=1), COL)
    hpht = jnp.sum(found[:, :, cols_dev:], axis=0)
    near = lax.dynamic_slice_in_dim(
        jnp.pad(found[:, :, :cols_dev], ((1, 1), (0, 0), (0, 0))), col, 3
    )
    hp = jnp.concatenate([near[0, :, cols_dev - margin :], near[1], near[2, :, :margin]], axis=1)
    hp = col_transported(hp, fields)

    block = jnp.concatenate([hp, hpht], axis=1)
    block = everyone(block, "z").reshape(nobs // 4, cols_dev + nobs)
    block = joined(block, lax.ppermute(block, "yl", SWAP), 0, lat_half)
    block = joined(block, lax.ppermute(block, "co", SWAP), 0, core)
    hp, hpht = block[:, :cols_dev], block[:, cols_dev:]

    inverse = spd_inverse(hpht, obs_var)
    pht = everyone(pht, COL).reshape(nobs, rows_dev)
    gain = dot(inverse, pht, (((1,), (0,)), ((), ())))
    return forecast - dot(gain, hp, (((0,), (0,)), ((), ())))


def solution(mesh):
    fine = Mesh(mesh.devices.reshape(2, 16, 2, 4, 4), ROW + COL)
    return jax.shard_map(
        shards,
        mesh=fine,
        in_specs=(P(ROW, COL), P(), P(), P(), P(), P(), P()),
        out_specs=P(ROW, COL),
        check_vma=False,
    )
```

```python
import functools

import jax
import jax.numpy as jnp
from jax import lax
from jax.experimental import pallas as pl
from jax.experimental.pallas import tpu as pltpu
from jax.sharding import Mesh
from jax.sharding import PartitionSpec as P

PARALLEL_STRIPS = 64
MERIDIAN_TOTAL = 128
STEPS = 3
HIGHEST = lax.Precision.HIGHEST
PANEL = 32
GROUP = 8
ROW = ("yl", "z", "co")
COL = ("yh", "x")


def padded_2(cells, sides, width):
    for axis, dim in sides:
        count = lax.axis_size(axis)
        ends = count - 1
        head = lax.slice_in_dim(cells, 0, width, axis=dim)
        tail = lax.slice_in_dim(cells, cells.shape[dim] - width, cells.shape[dim], axis=dim)
        cells = jnp.concatenate(
            [
                lax.ppermute(tail, axis, [(i, (i + 1) % count) for i in range(ends)]),
                cells,
                lax.ppermute(head, axis, [((i + 1) % count, i) for i in range(ends)]),
            ],
            axis=dim,
        )
    return cells


def advect(q, minus, plus, cu, cv, su, sv, lat_axis):
    lon_up = jnp.where(su > 0, jnp.roll(q, 1, lat_axis + 1), jnp.roll(q, -1, lat_axis + 1))
    lat_up = jnp.where(sv > 0, minus, plus)
    return q - cu * (q - lon_up) - cv * (q - lat_up)


def inverse_kernel(s_ref, var_ref, out_ref):
    n = s_ref.shape[0]
    s = s_ref[...]
    row_id = lax.broadcasted_iota(jnp.int32, (n, n), 0)
    col_id = lax.broadcasted_iota(jnp.int32, (n, n), 1)
    out_ref[...] = 0.5 * (s + s.T) + jnp.where(row_id == col_id, var_ref[...], 0.0)
    sub_wide = lax.broadcasted_iota(jnp.int32, (PANEL, n), 0)
    lane_wide = lax.broadcasted_iota(jnp.int32, (PANEL, n), 1)
    sub = lax.broadcasted_iota(jnp.int32, (PANEL, 128), 0)
    lane = lax.broadcasted_iota(jnp.int32, (PANEL, 128), 1)
    for at in range(0, n, PANEL):
        tile = at // 128 * 128
        rows = out_ref[at : at + PANEL, :]
        own = jnp.where(lane - (at - tile) == sub, 1.0, 0.0)
        for first in range(0, PANEL, GROUP):
            spread = [
                jnp.broadcast_to(rows[:, at + first + m : at + first + m + 1], (PANEL, 128))
                for m in range(GROUP)
            ]
            for m in range(GROUP):
                j = first + m
                factor = spread[m]
                pivot = factor[j : j + 1, :]
                inv = jnp.where(pivot > 0.0, 1.0 / pivot, jnp.nan)
                here = sub == j
                for k in range(m + 1, GROUP):
                    line = spread[k][j : j + 1, :] * inv
                    spread[k] = jnp.where(here, line, spread[k] - factor * line)
                line = own[j : j + 1, :] * inv
                own = jnp.where(here, line, own - factor * line)
                inv2 = jnp.concatenate([inv] * (n // 128), axis=1)
                factor2 = jnp.concatenate([factor] * (n // 128), axis=1)
                line = rows[j : j + 1, :] * inv2
                rows = jnp.where(sub_wide == j, line, rows - factor2 * line)
        placed = jnp.concatenate([own if t == tile else jnp.zeros_like(own) for t in range(0, n, 128)], axis=1)
        inside = (lane_wide >= at) & (lane_wide < at + PANEL)
        rows = jnp.where(inside, placed, rows)
        update = jnp.dot(out_ref[:, at : at + PANEL], rows, precision=HIGHEST, preferred_element_type=jnp.float32)
        keep = jnp.where((col_id >= at) & (col_id < at + PANEL), 0.0, out_ref[...])
        out_ref[...] = keep - update
        out_ref[at : at + PANEL, :] = rows


def spd_inverse(s, var):
    n = s.shape[0]
    return pl.pallas_call(
        inverse_kernel,
        out_shape=jax.ShapeDtypeStruct((n, n), jnp.float32),
        in_specs=[pl.BlockSpec(memory_space=pltpu.VMEM)] * 2,
        out_specs=pl.BlockSpec(memory_space=pltpu.VMEM),
        cost_estimate=pl.CostEstimate(flops=4 * n * n * n, bytes_accessed=8 * n * n, transcendentals=0),
        name="spd_inverse",
    )(s, var.reshape(1, n))


def footprint_kernel(start_ref, site_ref, cu_ref, cv_ref, su_ref, sv_ref, cov_ref, spread_ref, rows_ref, coef_ref, near_ref, site_col_ref):
    nobs = site_ref.shape[1]
    bands = cu_ref.shape[0]
    chunk = 32
    lane = lax.broadcasted_iota(jnp.int32, (chunk, MERIDIAN_TOTAL), 1)
    site_col_ref[...] = jnp.broadcast_to(site_ref[...], (8, nobs)).T

    def footprint(first, count, store):
        total = count + 2 * STEPS
        for t in range(total):
            band = first + (t - STEPS)
            inside = (band >= 0) & (band < bands)
            at = pl.ds(jnp.clip(band, 0, bands - 1), 1)
            cu = jnp.where(inside, cu_ref[at, :], 0.0)
            cv = jnp.where(inside, cv_ref[at, :], 0.0)
            west = jnp.where(su_ref[at, :] > 0, cu, 0.0)
            south = jnp.where(sv_ref[at, :] > 0, cv, 0.0)
            for k, line in enumerate((1.0 - cu - cv, west, cu - west, south, cv - south)):
                coef_ref[5 * t + k : 5 * t + k + 1, :] = line

        def coeff(t, k):
            return coef_ref[5 * t + k : 5 * t + k + 1, :]

        def body(i, carry):
            at = pl.multiple_of(i * chunk, chunk)
            site = site_col_ref[pl.ds(at, chunk), 0:1] - (first - STEPS) * MERIDIAN_TOTAL - lane
            v = [(site == t * MERIDIAN_TOTAL).astype(jnp.float32) for t in range(total)]
            for step in range(STEPS):
                low, high = (step + 1, total - step - 1)
                new = []
                for t in range(low, high):
                    w = coeff(t, 0) * v[t]
                    w = w + pltpu.roll(coeff(t, 1) * v[t], MERIDIAN_TOTAL - 1, 1)
                    w = w + pltpu.roll(coeff(t, 2) * v[t], 1, 1)
                    w = w + coeff(t + 1, 3) * v[t + 1]
                    w = w + coeff(t - 1, 4) * v[t - 1]
                    new.append(w)
                v = [None] * low + new + [None] * (total - high)
            store(at, v[STEPS : STEPS + count])
            return carry

        lax.fori_loop(0, nobs // chunk, body, 0)

    def store_near(at, v):
        near_ref[pl.ds(at, chunk), :] = v[0]

    def store_spread(at, v):
        for b, w in enumerate(v):
            spread_ref[pl.ds(at, chunk), b * MERIDIAN_TOTAL : (b + 1) * MERIDIAN_TOTAL] = w

    footprint(start_ref[0], 1, store_near)
    rows_ref[...] = jnp.dot(near_ref[...], cov_ref[...], precision=HIGHEST, preferred_element_type=jnp.float32)
    footprint(start_ref[1], cov_ref.shape[1] // MERIDIAN_TOTAL, store_spread)


def footprints(covariance, starts, site, *winds):
    rows_dev, cols_dev = covariance.shape
    assert rows_dev == MERIDIAN_TOTAL
    nobs = site.shape[0]
    bands = winds[0].shape[0] // MERIDIAN_TOTAL
    total = cols_dev // MERIDIAN_TOTAL + 2 * STEPS
    vmem = pl.BlockSpec(memory_space=pltpu.VMEM)
    return pl.pallas_call(
        footprint_kernel,
        out_shape=[jax.ShapeDtypeStruct((nobs, cols_dev), jnp.float32)] * 2,
        in_specs=[pl.BlockSpec(memory_space=pltpu.SMEM)] + [vmem] * 6,
        out_specs=[vmem] * 2,
        scratch_shapes=[
            pltpu.VMEM((5 * total + 6, MERIDIAN_TOTAL), jnp.float32),
            pltpu.VMEM((nobs, MERIDIAN_TOTAL), jnp.float32),
            pltpu.VMEM((nobs, 8), jnp.int32),
        ],
        cost_estimate=pl.CostEstimate(flops=400 * 1000 * 1000, bytes_accessed=1500000, transcendentals=0),
        name="footprints",
    )(starts, site.reshape(1, nobs), *(field.reshape(bands, MERIDIAN_TOTAL) for field in winds), covariance)


def everyone(chunk, axis):
    copies = jnp.broadcast_to(chunk, (lax.axis_size(axis), *chunk.shape))
    return lax.all_to_all(copies, axis, split_axis=0, concat_axis=0, tiled=True)


def scattered_sum(parts, axis):
    return jnp.sum(lax.all_to_all(parts, axis, split_axis=0, concat_axis=0, tiled=True), axis=0)


SWAP = [(0, 1), (1, 0)]


def halves(cells, dim, mine):
    width = cells.shape[dim] // 2
    low = lax.slice_in_dim(cells, 0, width, axis=dim)
    high = lax.slice_in_dim(cells, width, 2 * width, axis=dim)
    return jnp.where(mine == 0, low, high), jnp.where(mine == 0, high, low)


def joined(own, other, dim, mine):
    return jnp.concatenate(
        [jnp.where(mine == 0, own, other), jnp.where(mine == 0, other, own)], axis=dim
    )


def row_transported(cells, lon_speed, lat_speed, lon_sign, lat_sign, row_start):
    rows_dev, width = cells.shape
    row_bands = rows_dev // MERIDIAN_TOTAL

    def row_coeff(field):
        return lax.dynamic_slice_in_dim(field, row_start, rows_dev).reshape(
            row_bands, MERIDIAN_TOTAL, 1
        )

    row_cu, row_cv = (row_coeff(lon_speed), row_coeff(lat_speed))
    row_su, row_sv = (row_coeff(lon_sign), row_coeff(lat_sign))
    for step in range(STEPS):
        padded = padded_2(cells, ((ROW, 0),), MERIDIAN_TOTAL)
        shaped = padded.reshape(row_bands + 2, MERIDIAN_TOTAL, width)
        cells = advect(
            shaped[1:-1], shaped[:-2], shaped[2:], row_cu, row_cv, row_su, row_sv, 0
        )
        cells = cells.reshape(rows_dev, width)
    return cells


def col_fields(lon_speed, lat_speed, lon_sign, lat_sign, col_start, cols_dev):
    margin = STEPS * MERIDIAN_TOTAL
    total_bands = cols_dev // MERIDIAN_TOTAL + 2 * STEPS

    def wide_coeff(field):
        extended = jnp.pad(field, (margin, margin))
        return lax.dynamic_slice_in_dim(extended, col_start, cols_dev + 2 * margin).reshape(
            1, total_bands, MERIDIAN_TOTAL
        )

    band_ids = col_start // MERIDIAN_TOTAL - STEPS + jnp.arange(total_bands, dtype=jnp.int32)
    inside = (
        ((band_ids >= 0) & (band_ids < PARALLEL_STRIPS))
        .astype(jnp.float32)
        .reshape(1, total_bands, 1)
    )
    return [wide_coeff(field) for field in (lon_speed, lat_speed, lon_sign, lat_sign)] + [inside]


def col_transported(padded, fields):
    rows, width = padded.shape
    current = padded.reshape(rows, width // MERIDIAN_TOTAL, MERIDIAN_TOTAL)
    for step in range(STEPS):
        count = current.shape[1]
        low, high = (step + 1, step + count - 1)
        cu, cv, su, sv, inside = (field[:, low:high] for field in fields)
        current = (
            advect(current[:, 1:-1], current[:, :-2], current[:, 2:], cu, cv, su, sv, 1) * inside
        )
    return current.reshape(rows, -1)


def shards(
    covariance, lon_speed, lat_speed, lon_sign, lat_sign, measurement_site_position, obs_var
):
    rows_dev, cols_dev = covariance.shape
    nobs = measurement_site_position.shape[0]
    lat_half, core = lax.axis_index("yl"), lax.axis_index("co")
    row, col = lax.axis_index(ROW), lax.axis_index(COL)
    row_start, col_start = row * rows_dev, col * cols_dev
    margin = STEPS * MERIDIAN_TOTAL
    dot = functools.partial(
        lax.dot_general, precision=HIGHEST, preferred_element_type=jnp.float32
    )
    winds = (lon_speed, lat_speed, lon_sign, lat_sign)
    starts = jnp.stack([row_start, col_start]) // MERIDIAN_TOTAL
    spread, hp = footprints(covariance, starts, measurement_site_position, *winds)

    own, other = halves(hp, 0, core)
    own, other = halves(own + lax.ppermute(other, "co", SWAP), 0, lat_half)
    hp = own + lax.ppermute(other, "yl", SWAP)
    deep = lax.axis_size("z")
    hp = scattered_sum(hp.reshape(deep, nobs // 4 // deep, cols_dev), "z")

    forecast = row_transported(covariance, *winds, row_start)
    pht = dot(spread, forecast, (((1,), (1,)), ((), ())))
    fields = col_fields(*winds, col_start, cols_dev)

    sides = lax.axis_size(COL)
    hpht = dot(hp, spread, (((1,), (1,)), ((), ())))
    mine = jnp.concatenate([hp, hpht], axis=1)
    pht = pht.reshape(sides, nobs // sides, rows_dev)
    packed = jnp.broadcast_to(mine.reshape(1, -1, rows_dev), (sides, mine.size // rows_dev, rows_dev))
    packed = lax.all_to_all(
        jnp.concatenate([packed, pht], axis=1), COL, split_axis=0, concat_axis=0, tiled=True
    )
    found = packed[:, : mine.size // rows_dev].reshape(sides, *mine.shape)
    pht = jnp.sum(packed[:, mine.size // rows_dev :], axis=0)
    hpht = jnp.sum(found[:, :, cols_dev:], axis=0)
    near = lax.dynamic_slice_in_dim(
        jnp.pad(found[:, :, :cols_dev], ((1, 1), (0, 0), (0, 0))), col, 3
    )
    hp = jnp.concatenate([near[0, :, cols_dev - margin :], near[1], near[2, :, :margin]], axis=1)
    hp = col_transported(hp, fields)

    block = jnp.concatenate([hp, hpht], axis=1)
    block = everyone(block, "z").reshape(nobs // 4, cols_dev + nobs)
    forecast = col_transported(padded_2(forecast, ((COL, 1),), margin), fields)
    block = joined(block, lax.ppermute(block, "yl", SWAP), 0, lat_half)
    block = joined(block, lax.ppermute(block, "co", SWAP), 0, core)
    hp, hpht = block[:, :cols_dev], block[:, cols_dev:]

    pht, hpht = lax.optimization_barrier((pht, hpht))
    pht = everyone(pht, COL).reshape(nobs, rows_dev)
    inverse = spd_inverse(hpht, obs_var)
    gain = dot(inverse, pht, (((1,), (0,)), ((), ())))
    return forecast - dot(gain, hp, (((0,), (0,)), ((), ())))


def solution(mesh):
    fine = Mesh(mesh.devices.reshape(2, 16, 2, 4, 4), ROW + COL)
    return jax.shard_map(
        shards,
        mesh=fine,
        in_specs=(P(ROW, COL), P(), P(), P(), P(), P(), P()),
        out_specs=P(ROW, COL),
        check_vma=False,
    )
```

```python
import functools

import jax
import jax.numpy as jnp
from jax import lax
from jax.experimental import pallas as pl
from jax.experimental.pallas import tpu as pltpu
from jax.sharding import Mesh
from jax.sharding import PartitionSpec as P

PARALLEL_STRIPS = 64
MERIDIAN_TOTAL = 128
STEPS = 3
HIGHEST = lax.Precision.HIGHEST
PANEL = 32
GROUP = 8
ROW = ("yl", "z", "co")
COL = ("yh", "x")


def padded_2(cells, sides, width):
    for axis, dim in sides:
        count = lax.axis_size(axis)
        ends = count - 1
        head = lax.slice_in_dim(cells, 0, width, axis=dim)
        tail = lax.slice_in_dim(cells, cells.shape[dim] - width, cells.shape[dim], axis=dim)
        cells = jnp.concatenate(
            [
                lax.ppermute(tail, axis, [(i, (i + 1) % count) for i in range(ends)]),
                cells,
                lax.ppermute(head, axis, [((i + 1) % count, i) for i in range(ends)]),
            ],
            axis=dim,
        )
    return cells


def advect(q, minus, plus, cu, cv, su, sv, lat_axis):
    lon_up = jnp.where(su > 0, jnp.roll(q, 1, lat_axis + 1), jnp.roll(q, -1, lat_axis + 1))
    lat_up = jnp.where(sv > 0, minus, plus)
    return q - cu * (q - lon_up) - cv * (q - lat_up)


def inverse_kernel(s_ref, var_ref, out_ref):
    n = s_ref.shape[0]
    s = s_ref[...]
    row_id = lax.broadcasted_iota(jnp.int32, (n, n), 0)
    col_id = lax.broadcasted_iota(jnp.int32, (n, n), 1)
    out_ref[...] = 0.5 * (s + s.T) + jnp.where(row_id == col_id, var_ref[...], 0.0)
    sub_wide = lax.broadcasted_iota(jnp.int32, (PANEL, n), 0)
    lane_wide = lax.broadcasted_iota(jnp.int32, (PANEL, n), 1)
    sub = lax.broadcasted_iota(jnp.int32, (PANEL, 128), 0)
    lane = lax.broadcasted_iota(jnp.int32, (PANEL, 128), 1)
    for at in range(0, n, PANEL):
        tile = at // 128 * 128
        rows = out_ref[at : at + PANEL, :]
        own = jnp.where(lane - (at - tile) == sub, 1.0, 0.0)
        for first in range(0, PANEL, GROUP):
            spread = [
                jnp.broadcast_to(rows[:, at + first + m : at + first + m + 1], (PANEL, 128))
                for m in range(GROUP)
            ]
            for m in range(GROUP):
                j = first + m
                factor = spread[m]
                pivot = factor[j : j + 1, :]
                inv = jnp.where(pivot > 0.0, 1.0 / pivot, jnp.nan)
                here = sub == j
                for k in range(m + 1, GROUP):
                    line = spread[k][j : j + 1, :] * inv
                    spread[k] = jnp.where(here, line, spread[k] - factor * line)
                line = own[j : j + 1, :] * inv
                own = jnp.where(here, line, own - factor * line)
                inv2 = jnp.concatenate([inv] * (n // 128), axis=1)
                factor2 = jnp.concatenate([factor] * (n // 128), axis=1)
                line = rows[j : j + 1, :] * inv2
                rows = jnp.where(sub_wide == j, line, rows - factor2 * line)
        placed = jnp.concatenate([own if t == tile else jnp.zeros_like(own) for t in range(0, n, 128)], axis=1)
        inside = (lane_wide >= at) & (lane_wide < at + PANEL)
        rows = jnp.where(inside, placed, rows)
        update = jnp.dot(out_ref[:, at : at + PANEL], rows, precision=HIGHEST, preferred_element_type=jnp.float32)
        keep = jnp.where((col_id >= at) & (col_id < at + PANEL), 0.0, out_ref[...])
        out_ref[...] = keep - update
        out_ref[at : at + PANEL, :] = rows


def spd_inverse(s, var):
    n = s.shape[0]
    return pl.pallas_call(
        inverse_kernel,
        out_shape=jax.ShapeDtypeStruct((n, n), jnp.float32),
        in_specs=[pl.BlockSpec(memory_space=pltpu.VMEM)] * 2,
        out_specs=pl.BlockSpec(memory_space=pltpu.VMEM),
        cost_estimate=pl.CostEstimate(flops=4 * n * n * n, bytes_accessed=8 * n * n, transcendentals=0),
        name="spd_inverse",
    )(s, var.reshape(1, n))


def footprint_kernel(start_ref, site_ref, cu_ref, cv_ref, su_ref, sv_ref, cov_ref, spread_ref, rows_ref, coef_ref, near_ref, site_col_ref):
    nobs = site_ref.shape[1]
    bands = cu_ref.shape[0]
    chunk = 32
    lane = lax.broadcasted_iota(jnp.int32, (chunk, MERIDIAN_TOTAL), 1)
    site_col_ref[...] = jnp.broadcast_to(site_ref[...], (8, nobs)).T

    def footprint(first, count, store):
        total = count + 2 * STEPS
        for t in range(total):
            band = first + (t - STEPS)
            inside = (band >= 0) & (band < bands)
            at = pl.ds(jnp.clip(band, 0, bands - 1), 1)
            cu = jnp.where(inside, cu_ref[at, :], 0.0)
            cv = jnp.where(inside, cv_ref[at, :], 0.0)
            west = jnp.where(su_ref[at, :] > 0, cu, 0.0)
            south = jnp.where(sv_ref[at, :] > 0, cv, 0.0)
            for k, line in enumerate((1.0 - cu - cv, west, cu - west, south, cv - south)):
                coef_ref[5 * t + k : 5 * t + k + 1, :] = line

        def coeff(t, k):
            return coef_ref[5 * t + k : 5 * t + k + 1, :]

        def body(i, carry):
            at = pl.multiple_of(i * chunk, chunk)
            site = site_col_ref[pl.ds(at, chunk), 0:1] - (first - STEPS) * MERIDIAN_TOTAL - lane
            v = [(site == t * MERIDIAN_TOTAL).astype(jnp.float32) for t in range(total)]
            for step in range(STEPS):
                low, high = (step + 1, total - step - 1)
                new = []
                for t in range(low, high):
                    w = coeff(t, 0) * v[t]
                    w = w + pltpu.roll(coeff(t, 1) * v[t], MERIDIAN_TOTAL - 1, 1)
                    w = w + pltpu.roll(coeff(t, 2) * v[t], 1, 1)
                    w = w + coeff(t + 1, 3) * v[t + 1]
                    w = w + coeff(t - 1, 4) * v[t - 1]
                    new.append(w)
                v = [None] * low + new + [None] * (total - high)
            store(at, v[STEPS : STEPS + count])
            return carry

        lax.fori_loop(0, nobs // chunk, body, 0)

    def store_near(at, v):
        near_ref[pl.ds(at, chunk), :] = v[0]

    def store_spread(at, v):
        for b, w in enumerate(v):
            spread_ref[pl.ds(at, chunk), b * MERIDIAN_TOTAL : (b + 1) * MERIDIAN_TOTAL] = w

    footprint(start_ref[0], 1, store_near)
    rows_ref[...] = jnp.dot(near_ref[...], cov_ref[...], precision=HIGHEST, preferred_element_type=jnp.float32)
    footprint(start_ref[1], cov_ref.shape[1] // MERIDIAN_TOTAL, store_spread)


def footprints(covariance, starts, site, *winds):
    rows_dev, cols_dev = covariance.shape
    assert rows_dev == MERIDIAN_TOTAL
    nobs = site.shape[0]
    bands = winds[0].shape[0] // MERIDIAN_TOTAL
    total = cols_dev // MERIDIAN_TOTAL + 2 * STEPS
    vmem = pl.BlockSpec(memory_space=pltpu.VMEM)
    return pl.pallas_call(
        footprint_kernel,
        out_shape=[jax.ShapeDtypeStruct((nobs, cols_dev), jnp.float32)] * 2,
        in_specs=[pl.BlockSpec(memory_space=pltpu.SMEM)] + [vmem] * 6,
        out_specs=[vmem] * 2,
        scratch_shapes=[
            pltpu.VMEM((5 * total + 6, MERIDIAN_TOTAL), jnp.float32),
            pltpu.VMEM((nobs, MERIDIAN_TOTAL), jnp.float32),
            pltpu.VMEM((nobs, 8), jnp.int32),
        ],
        cost_estimate=pl.CostEstimate(flops=400 * 1000 * 1000, bytes_accessed=1500000, transcendentals=0),
        name="footprints",
    )(starts, site.reshape(1, nobs), *(field.reshape(bands, MERIDIAN_TOTAL) for field in winds), covariance)


def everyone(chunk, axis):
    copies = jnp.broadcast_to(chunk, (lax.axis_size(axis), *chunk.shape))
    return lax.all_to_all(copies, axis, split_axis=0, concat_axis=0, tiled=True)


def scattered_sum(parts, axis):
    return jnp.sum(lax.all_to_all(parts, axis, split_axis=0, concat_axis=0, tiled=True), axis=0)


SWAP = [(0, 1), (1, 0)]


def halves(cells, dim, mine):
    width = cells.shape[dim] // 2
    low = lax.slice_in_dim(cells, 0, width, axis=dim)
    high = lax.slice_in_dim(cells, width, 2 * width, axis=dim)
    return jnp.where(mine == 0, low, high), jnp.where(mine == 0, high, low)


def joined(own, other, dim, mine):
    return jnp.concatenate(
        [jnp.where(mine == 0, own, other), jnp.where(mine == 0, other, own)], axis=dim
    )


def row_transported(cells, lon_speed, lat_speed, lon_sign, lat_sign, row_start):
    rows_dev, width = cells.shape
    row_bands = rows_dev // MERIDIAN_TOTAL

    def row_coeff(field):
        return lax.dynamic_slice_in_dim(field, row_start, rows_dev).reshape(
            row_bands, MERIDIAN_TOTAL, 1
        )

    row_cu, row_cv = (row_coeff(lon_speed), row_coeff(lat_speed))
    row_su, row_sv = (row_coeff(lon_sign), row_coeff(lat_sign))
    for _ in range(STEPS):
        padded = padded_2(cells, ((ROW, 0),), MERIDIAN_TOTAL)
        shaped = padded.reshape(row_bands + 2, MERIDIAN_TOTAL, width)
        cells = advect(
            shaped[1:-1], shaped[:-2], shaped[2:], row_cu, row_cv, row_su, row_sv, 0
        )
        cells = cells.reshape(rows_dev, width)
    return cells


def col_fields(lon_speed, lat_speed, lon_sign, lat_sign, col_start, cols_dev):
    margin = STEPS * MERIDIAN_TOTAL
    total_bands = cols_dev // MERIDIAN_TOTAL + 2 * STEPS

    def wide_coeff(field):
        extended = jnp.pad(field, (margin, margin))
        return lax.dynamic_slice_in_dim(extended, col_start, cols_dev + 2 * margin).reshape(
            1, total_bands, MERIDIAN_TOTAL
        )

    band_ids = col_start // MERIDIAN_TOTAL - STEPS + jnp.arange(total_bands, dtype=jnp.int32)
    inside = (
        ((band_ids >= 0) & (band_ids < PARALLEL_STRIPS))
        .astype(jnp.float32)
        .reshape(1, total_bands, 1)
    )
    return [wide_coeff(field) for field in (lon_speed, lat_speed, lon_sign, lat_sign)] + [inside]


def col_transported(padded, fields):
    rows, width = padded.shape
    current = padded.reshape(rows, width // MERIDIAN_TOTAL, MERIDIAN_TOTAL)
    for step in range(STEPS):
        count = current.shape[1]
        low, high = (step + 1, step + count - 1)
        cu, cv, su, sv, inside = (field[:, low:high] for field in fields)
        current = (
            advect(current[:, 1:-1], current[:, :-2], current[:, 2:], cu, cv, su, sv, 1) * inside
        )
    return current.reshape(rows, -1)


def shards(
    covariance, lon_speed, lat_speed, lon_sign, lat_sign, measurement_site_position, obs_var
):
    rows_dev, cols_dev = covariance.shape
    nobs = measurement_site_position.shape[0]
    lat_half, core = lax.axis_index("yl"), lax.axis_index("co")
    row, col = lax.axis_index(ROW), lax.axis_index(COL)
    row_start, col_start = row * rows_dev, col * cols_dev
    margin = STEPS * MERIDIAN_TOTAL
    dot = functools.partial(
        lax.dot_general, precision=HIGHEST, preferred_element_type=jnp.float32
    )
    winds = (lon_speed, lat_speed, lon_sign, lat_sign)
    starts = jnp.stack([row_start, col_start]) // MERIDIAN_TOTAL
    spread, hp = footprints(covariance, starts, measurement_site_position, *winds)

    own, other = halves(hp, 0, core)
    own, other = halves(own + lax.ppermute(other, "co", SWAP), 0, lat_half)
    hp = own + lax.ppermute(other, "yl", SWAP)
    deep = lax.axis_size("z")
    hp = scattered_sum(hp.reshape(deep, nobs // 4 // deep, cols_dev), "z")

    forecast = row_transported(covariance, *winds, row_start)
    pht = dot(spread, forecast, (((1,), (1,)), ((), ())))
    fields = col_fields(*winds, col_start, cols_dev)

    sides = lax.axis_size(COL)
    hpht = dot(hp, spread, (((1,), (1,)), ((), ())))
    mine = jnp.concatenate([hp, hpht], axis=1)
    pht = pht.reshape(sides, nobs // sides, rows_dev)
    packed = jnp.broadcast_to(mine.reshape(1, -1, rows_dev), (sides, mine.size // rows_dev, rows_dev))
    packed = lax.all_to_all(
        jnp.concatenate([packed, pht], axis=1), COL, split_axis=0, concat_axis=0, tiled=True
    )
    packed, forecast = lax.optimization_barrier((packed, forecast))
    found = packed[:, : mine.size // rows_dev].reshape(sides, *mine.shape)
    pht = jnp.sum(packed[:, mine.size // rows_dev :], axis=0)
    hpht = jnp.sum(found[:, :, cols_dev:], axis=0)
    near = lax.dynamic_slice_in_dim(
        jnp.pad(found[:, :, :cols_dev], ((1, 1), (0, 0), (0, 0))), col, 3
    )
    hp = jnp.concatenate([near[0, :, cols_dev - margin :], near[1], near[2, :, :margin]], axis=1)
    hp = col_transported(hp, fields)

    block = jnp.concatenate([hp, hpht], axis=1)
    block = everyone(block, "z").reshape(nobs // 4, cols_dev + nobs)
    forecast = padded_2(forecast, ((COL, 1),), margin)
    forecast = col_transported(forecast, fields)
    block = joined(block, lax.ppermute(block, "yl", SWAP), 0, lat_half)
    block = joined(block, lax.ppermute(block, "co", SWAP), 0, core)
    hp, hpht = block[:, :cols_dev], block[:, cols_dev:]

    pht, hpht = lax.optimization_barrier((pht, hpht))
    pht = everyone(pht, COL).reshape(nobs, rows_dev)
    inverse = spd_inverse(hpht, obs_var)
    gain = dot(inverse, pht, (((1,), (0,)), ((), ())))
    return forecast - dot(gain, hp, (((0,), (0,)), ((), ())))


def solution(mesh):
    fine = Mesh(mesh.devices.reshape(2, 16, 2, 4, 4), ROW + COL)
    return jax.shard_map(
        shards,
        mesh=fine,
        in_specs=(P(ROW, COL), P(), P(), P(), P(), P(), P()),
        out_specs=P(ROW, COL),
        check_vma=False,
    )
```

```python
import functools

import jax
import jax.numpy as jnp
from jax import lax
from jax.experimental import pallas as pl
from jax.experimental.pallas import tpu as pltpu
from jax.sharding import Mesh
from jax.sharding import PartitionSpec as P

PARALLEL_STRIPS = 64
MERIDIAN_TOTAL = 128
STEPS = 3
HIGHEST = lax.Precision.HIGHEST
PANEL = 32
GROUP = 8
ROW = ("yl", "z", "co")
COL = ("yh", "x")


def padded_2(cells, sides, width):
    for axis, dim in sides:
        count = lax.axis_size(axis)
        ends = count - 1
        head = lax.slice_in_dim(cells, 0, width, axis=dim)
        tail = lax.slice_in_dim(cells, cells.shape[dim] - width, cells.shape[dim], axis=dim)
        cells = jnp.concatenate(
            [
                lax.ppermute(tail, axis, [(i, (i + 1) % count) for i in range(ends)]),
                cells,
                lax.ppermute(head, axis, [((i + 1) % count, i) for i in range(ends)]),
            ],
            axis=dim,
        )
    return cells


def advect(q, minus, plus, cu, cv, su, sv, lat_axis):
    lon_up = jnp.where(su > 0, jnp.roll(q, 1, lat_axis + 1), jnp.roll(q, -1, lat_axis + 1))
    lat_up = jnp.where(sv > 0, minus, plus)
    return q - cu * (q - lon_up) - cv * (q - lat_up)


def inverse_kernel(s_ref, var_ref, out_ref):
    n = s_ref.shape[0]
    s = s_ref[...]
    row_id = lax.broadcasted_iota(jnp.int32, (n, n), 0)
    col_id = lax.broadcasted_iota(jnp.int32, (n, n), 1)
    out_ref[...] = 0.5 * (s + s.T) + jnp.where(row_id == col_id, var_ref[...], 0.0)
    sub_wide = lax.broadcasted_iota(jnp.int32, (PANEL, n), 0)
    lane_wide = lax.broadcasted_iota(jnp.int32, (PANEL, n), 1)
    sub = lax.broadcasted_iota(jnp.int32, (PANEL, 128), 0)
    lane = lax.broadcasted_iota(jnp.int32, (PANEL, 128), 1)
    for at in range(0, n, PANEL):
        tile = at // 128 * 128
        rows = out_ref[at : at + PANEL, :]
        own = jnp.where(lane - (at - tile) == sub, 1.0, 0.0)
        for first in range(0, PANEL, GROUP):
            spread = [
                jnp.broadcast_to(rows[:, at + first + m : at + first + m + 1], (PANEL, 128))
                for m in range(GROUP)
            ]
            for m in range(GROUP):
                j = first + m
                factor = spread[m]
                pivot = factor[j : j + 1, :]
                inv = jnp.where(pivot > 0.0, 1.0 / pivot, jnp.nan)
                here = sub == j
                for k in range(m + 1, GROUP):
                    line = spread[k][j : j + 1, :] * inv
                    spread[k] = jnp.where(here, line, spread[k] - factor * line)
                line = own[j : j + 1, :] * inv
                own = jnp.where(here, line, own - factor * line)
                inv2 = jnp.concatenate([inv] * (n // 128), axis=1)
                factor2 = jnp.concatenate([factor] * (n // 128), axis=1)
                line = rows[j : j + 1, :] * inv2
                rows = jnp.where(sub_wide == j, line, rows - factor2 * line)
        placed = jnp.concatenate([own if t == tile else jnp.zeros_like(own) for t in range(0, n, 128)], axis=1)
        inside = (lane_wide >= at) & (lane_wide < at + PANEL)
        rows = jnp.where(inside, placed, rows)
        update = jnp.dot(out_ref[:, at : at + PANEL], rows, precision=HIGHEST, preferred_element_type=jnp.float32)
        keep = jnp.where((col_id >= at) & (col_id < at + PANEL), 0.0, out_ref[...])
        out_ref[...] = keep - update
        out_ref[at : at + PANEL, :] = rows


def spd_inverse(s, var):
    n = s.shape[0]
    return pl.pallas_call(
        inverse_kernel,
        out_shape=jax.ShapeDtypeStruct((n, n), jnp.float32),
        in_specs=[pl.BlockSpec(memory_space=pltpu.VMEM)] * 2,
        out_specs=pl.BlockSpec(memory_space=pltpu.VMEM),
        cost_estimate=pl.CostEstimate(flops=4 * n * n * n, bytes_accessed=8 * n * n, transcendentals=0),
        name="spd_inverse",
    )(s, var.reshape(1, n))


def footprint(start_ref, site_ref, cu_ref, cv_ref, su_ref, sv_ref, out_ref, coef_ref, site_col_ref):
    nobs = site_ref.shape[1]
    bands = cu_ref.shape[0]
    count = out_ref.shape[1] // MERIDIAN_TOTAL
    total = count + 2 * STEPS
    first = start_ref[0]
    chunk = 32
    lane = lax.broadcasted_iota(jnp.int32, (chunk, MERIDIAN_TOTAL), 1)
    site_col_ref[...] = jnp.broadcast_to(site_ref[...], (8, nobs)).T
    for t in range(total):
        band = first + (t - STEPS)
        inside = (band >= 0) & (band < bands)
        at = pl.ds(jnp.clip(band, 0, bands - 1), 1)
        cu = jnp.where(inside, cu_ref[at, :], 0.0)
        cv = jnp.where(inside, cv_ref[at, :], 0.0)
        west = jnp.where(su_ref[at, :] > 0, cu, 0.0)
        south = jnp.where(sv_ref[at, :] > 0, cv, 0.0)
        for k, line in enumerate((1.0 - cu - cv, west, cu - west, south, cv - south)):
            coef_ref[5 * t + k : 5 * t + k + 1, :] = line

    def coeff(t, k):
        return coef_ref[5 * t + k : 5 * t + k + 1, :]

    def body(i, carry):
        at = pl.multiple_of(i * chunk, chunk)
        site = site_col_ref[pl.ds(at, chunk), 0:1] - (first - STEPS) * MERIDIAN_TOTAL - lane
        v = [(site == t * MERIDIAN_TOTAL).astype(jnp.float32) for t in range(total)]
        for step in range(STEPS):
            low, high = (step + 1, total - step - 1)
            new = []
            for t in range(low, high):
                w = coeff(t, 0) * v[t]
                w = w + pltpu.roll(coeff(t, 1) * v[t], MERIDIAN_TOTAL - 1, 1)
                w = w + pltpu.roll(coeff(t, 2) * v[t], 1, 1)
                w = w + coeff(t + 1, 3) * v[t + 1]
                w = w + coeff(t - 1, 4) * v[t - 1]
                new.append(w)
            v = [None] * low + new + [None] * (total - high)
        for b in range(count):
            out_ref[pl.ds(at, chunk), b * MERIDIAN_TOTAL : (b + 1) * MERIDIAN_TOTAL] = v[STEPS + b]
        return carry

    lax.fori_loop(0, nobs // chunk, body, 0)


def rows_kernel(start_ref, site_ref, cu_ref, cv_ref, su_ref, sv_ref, cov_ref, rows_ref, near_ref, coef_ref, site_col_ref):
    footprint(start_ref, site_ref, cu_ref, cv_ref, su_ref, sv_ref, near_ref, coef_ref, site_col_ref)
    rows_ref[...] = jnp.dot(near_ref[...], cov_ref[...], precision=HIGHEST, preferred_element_type=jnp.float32)


def footprint_call(kernel, cells, nobs, width, scratch, operands):
    vmem = pl.BlockSpec(memory_space=pltpu.VMEM)
    total = cells // MERIDIAN_TOTAL + 2 * STEPS
    return pl.pallas_call(
        kernel,
        out_shape=jax.ShapeDtypeStruct((nobs, width), jnp.float32),
        in_specs=[pl.BlockSpec(memory_space=pltpu.SMEM)] + [vmem] * (len(operands) - 1),
        out_specs=vmem,
        scratch_shapes=[
            *scratch,
            pltpu.VMEM((5 * total + 6, MERIDIAN_TOTAL), jnp.float32),
            pltpu.VMEM((nobs, 8), jnp.int32),
        ],
        cost_estimate=pl.CostEstimate(flops=200 * 1000 * 1000, bytes_accessed=900000, transcendentals=0),
    )(*operands)


def gridded(site, winds):
    return [site.reshape(1, -1)] + [field.reshape(-1, MERIDIAN_TOTAL) for field in winds]


def observed_rows(covariance, band, site, *winds):
    rows_dev, cols_dev = covariance.shape
    assert rows_dev == MERIDIAN_TOTAL
    nobs = site.shape[0]
    operands = [band.reshape(1), *gridded(site, winds), covariance]
    near = [pltpu.VMEM((nobs, rows_dev), jnp.float32)]
    return footprint_call(rows_kernel, rows_dev, nobs, cols_dev, near, operands)


def column_footprint(cols_dev, band, site, *winds):
    operands = [band.reshape(1), *gridded(site, winds)]
    return footprint_call(footprint, cols_dev, site.shape[0], cols_dev, [], operands)


def everyone(chunk, axis):
    copies = jnp.broadcast_to(chunk, (lax.axis_size(axis), *chunk.shape))
    return lax.all_to_all(copies, axis, split_axis=0, concat_axis=0, tiled=True)


def scattered_sum(parts, axis):
    return jnp.sum(lax.all_to_all(parts, axis, split_axis=0, concat_axis=0, tiled=True), axis=0)


SWAP = [(0, 1), (1, 0)]


def halves(cells, dim, mine):
    width = cells.shape[dim] // 2
    low = lax.slice_in_dim(cells, 0, width, axis=dim)
    high = lax.slice_in_dim(cells, width, 2 * width, axis=dim)
    return jnp.where(mine == 0, low, high), jnp.where(mine == 0, high, low)


def joined(own, other, dim, mine):
    return jnp.concatenate(
        [jnp.where(mine == 0, own, other), jnp.where(mine == 0, other, own)], axis=dim
    )


def row_transported(cells, lon_speed, lat_speed, lon_sign, lat_sign, row_start):
    rows_dev, width = cells.shape
    row_bands = rows_dev // MERIDIAN_TOTAL

    def row_coeff(field):
        return lax.dynamic_slice_in_dim(field, row_start, rows_dev).reshape(
            row_bands, MERIDIAN_TOTAL, 1
        )

    row_cu, row_cv = (row_coeff(lon_speed), row_coeff(lat_speed))
    row_su, row_sv = (row_coeff(lon_sign), row_coeff(lat_sign))
    for _ in range(STEPS):
        padded = padded_2(cells, ((ROW, 0),), MERIDIAN_TOTAL)
        shaped = padded.reshape(row_bands + 2, MERIDIAN_TOTAL, width)
        cells = advect(
            shaped[1:-1], shaped[:-2], shaped[2:], row_cu, row_cv, row_su, row_sv, 0
        )
        cells = cells.reshape(rows_dev, width)
    return cells


def col_fields(lon_speed, lat_speed, lon_sign, lat_sign, col_start, cols_dev):
    margin = STEPS * MERIDIAN_TOTAL
    total_bands = cols_dev // MERIDIAN_TOTAL + 2 * STEPS

    def wide_coeff(field):
        extended = jnp.pad(field, (margin, margin))
        return lax.dynamic_slice_in_dim(extended, col_start, cols_dev + 2 * margin).reshape(
            1, total_bands, MERIDIAN_TOTAL
        )

    band_ids = col_start // MERIDIAN_TOTAL - STEPS + jnp.arange(total_bands, dtype=jnp.int32)
    inside = (
        ((band_ids >= 0) & (band_ids < PARALLEL_STRIPS))
        .astype(jnp.float32)
        .reshape(1, total_bands, 1)
    )
    return [wide_coeff(field) for field in (lon_speed, lat_speed, lon_sign, lat_sign)] + [inside]


def col_transported(padded, fields):
    rows, width = padded.shape
    current = padded.reshape(rows, width // MERIDIAN_TOTAL, MERIDIAN_TOTAL)
    for step in range(STEPS):
        count = current.shape[1]
        low, high = (step + 1, step + count - 1)
        cu, cv, su, sv, inside = (field[:, low:high] for field in fields)
        current = (
            advect(current[:, 1:-1], current[:, :-2], current[:, 2:], cu, cv, su, sv, 1) * inside
        )
    return current.reshape(rows, -1)


def shards(
    covariance, lon_speed, lat_speed, lon_sign, lat_sign, measurement_site_position, obs_var
):
    rows_dev, cols_dev = covariance.shape
    nobs = measurement_site_position.shape[0]
    lat_half, core = lax.axis_index("yl"), lax.axis_index("co")
    row, col = lax.axis_index(ROW), lax.axis_index(COL)
    row_start, col_start = row * rows_dev, col * cols_dev
    margin = STEPS * MERIDIAN_TOTAL
    dot = functools.partial(
        lax.dot_general, precision=HIGHEST, preferred_element_type=jnp.float32
    )
    winds = (lon_speed, lat_speed, lon_sign, lat_sign)
    hp = observed_rows(
        covariance, row_start // MERIDIAN_TOTAL, measurement_site_position, *winds
    )
    spread = column_footprint(
        cols_dev, col_start // MERIDIAN_TOTAL, measurement_site_position, *winds
    )

    own, other = halves(hp, 0, core)
    fellow = lax.ppermute(other, "co", SWAP)
    own, other = halves(own + fellow, 0, lat_half)
    fellow = lax.ppermute(other, "yl", SWAP)
    hp = own + fellow
    deep = lax.axis_size("z")
    hp = scattered_sum(hp.reshape(deep, nobs // 4 // deep, cols_dev), "z")

    forecast = row_transported(covariance, *winds, row_start)
    pht = dot(spread, forecast, (((1,), (1,)), ((), ())))
    fields = col_fields(*winds, col_start, cols_dev)

    sides = lax.axis_size(COL)
    hpht = dot(hp, spread, (((1,), (1,)), ((), ())))
    mine = jnp.concatenate([hp, hpht], axis=1)
    pht = pht.reshape(sides, nobs // sides, rows_dev)
    packed = jnp.broadcast_to(mine.reshape(1, -1, rows_dev), (sides, mine.size // rows_dev, rows_dev))
    packed = lax.all_to_all(
        jnp.concatenate([packed, pht], axis=1), COL, split_axis=0, concat_axis=0, tiled=True
    )
    packed, forecast = lax.optimization_barrier((packed, forecast))
    found = packed[:, : mine.size // rows_dev].reshape(sides, *mine.shape)
    pht = jnp.sum(packed[:, mine.size // rows_dev :], axis=0)
    hpht = jnp.sum(found[:, :, cols_dev:], axis=0)
    near = lax.dynamic_slice_in_dim(
        jnp.pad(found[:, :, :cols_dev], ((1, 1), (0, 0), (0, 0))), col, 3
    )
    hp = jnp.concatenate([near[0, :, cols_dev - margin :], near[1], near[2, :, :margin]], axis=1)
    hp = col_transported(hp, fields)

    block = jnp.concatenate([hp, hpht], axis=1)
    block = everyone(block, "z").reshape(nobs // 4, cols_dev + nobs)
    forecast = padded_2(forecast, ((COL, 1),), margin)
    forecast = col_transported(forecast, fields)
    block = joined(block, lax.ppermute(block, "yl", SWAP), 0, lat_half)
    block = joined(block, lax.ppermute(block, "co", SWAP), 0, core)
    hp, hpht = block[:, :cols_dev], block[:, cols_dev:]

    pht, hpht = lax.optimization_barrier((pht, hpht))
    pht = everyone(pht, COL).reshape(nobs, rows_dev)
    inverse = spd_inverse(hpht, obs_var)
    gain = dot(inverse, pht, (((1,), (0,)), ((), ())))
    return forecast - dot(gain, hp, (((0,), (0,)), ((), ())))


def solution(mesh):
    fine = Mesh(mesh.devices.reshape(2, 16, 2, 4, 4), ROW + COL)
    return jax.shard_map(
        shards,
        mesh=fine,
        in_specs=(P(ROW, COL), P(), P(), P(), P(), P(), P()),
        out_specs=P(ROW, COL),
        check_vma=False,
    )
```

```python
import functools

import jax
import jax.numpy as jnp
from jax import lax
from jax.experimental import pallas as pl
from jax.experimental.pallas import tpu as pltpu
from jax.sharding import Mesh
from jax.sharding import PartitionSpec as P

PARALLEL_STRIPS = 64
MERIDIAN_TOTAL = 128
STEPS = 3
HIGHEST = lax.Precision.HIGHEST
PANEL = 32
GROUP = 8
ROW = ("yl", "z", "co")
COL = ("yh", "x")


def padded_2(cells, sides, width):
    for axis, dim in sides:
        count = lax.axis_size(axis)
        ends = count - 1
        head = lax.slice_in_dim(cells, 0, width, axis=dim)
        tail = lax.slice_in_dim(cells, cells.shape[dim] - width, cells.shape[dim], axis=dim)
        cells = jnp.concatenate(
            [
                lax.ppermute(tail, axis, [(i, (i + 1) % count) for i in range(ends)]),
                cells,
                lax.ppermute(head, axis, [((i + 1) % count, i) for i in range(ends)]),
            ],
            axis=dim,
        )
    return cells


def advect(q, minus, plus, cu, cv, su, sv, lat_axis):
    lon_up = jnp.where(su > 0, jnp.roll(q, 1, lat_axis + 1), jnp.roll(q, -1, lat_axis + 1))
    lat_up = jnp.where(sv > 0, minus, plus)
    return q - cu * (q - lon_up) - cv * (q - lat_up)


def inverse_kernel(s_ref, var_ref, out_ref):
    n = s_ref.shape[0]
    s = s_ref[...]
    row_id = lax.broadcasted_iota(jnp.int32, (n, n), 0)
    col_id = lax.broadcasted_iota(jnp.int32, (n, n), 1)
    out_ref[...] = 0.5 * (s + s.T) + jnp.where(row_id == col_id, var_ref[...], 0.0)
    sub_wide = lax.broadcasted_iota(jnp.int32, (PANEL, n), 0)
    lane_wide = lax.broadcasted_iota(jnp.int32, (PANEL, n), 1)
    sub = lax.broadcasted_iota(jnp.int32, (PANEL, 128), 0)
    lane = lax.broadcasted_iota(jnp.int32, (PANEL, 128), 1)
    for at in range(0, n, PANEL):
        tile = at // 128 * 128
        rows = out_ref[at : at + PANEL, :]
        own = jnp.where(lane - (at - tile) == sub, 1.0, 0.0)
        for first in range(0, PANEL, GROUP):
            spread = [
                jnp.broadcast_to(rows[:, at + first + m : at + first + m + 1], (PANEL, 128))
                for m in range(GROUP)
            ]
            for m in range(GROUP):
                j = first + m
                factor = spread[m]
                pivot = factor[j : j + 1, :]
                inv = jnp.where(pivot > 0.0, 1.0 / pivot, jnp.nan)
                here = sub == j
                for k in range(m + 1, GROUP):
                    line = spread[k][j : j + 1, :] * inv
                    spread[k] = jnp.where(here, line, spread[k] - factor * line)
                line = own[j : j + 1, :] * inv
                own = jnp.where(here, line, own - factor * line)
                inv2 = jnp.concatenate([inv] * (n // 128), axis=1)
                factor2 = jnp.concatenate([factor] * (n // 128), axis=1)
                line = rows[j : j + 1, :] * inv2
                rows = jnp.where(sub_wide == j, line, rows - factor2 * line)
        placed = jnp.concatenate([own if t == tile else jnp.zeros_like(own) for t in range(0, n, 128)], axis=1)
        inside = (lane_wide >= at) & (lane_wide < at + PANEL)
        rows = jnp.where(inside, placed, rows)
        update = jnp.dot(out_ref[:, at : at + PANEL], rows, precision=HIGHEST, preferred_element_type=jnp.float32)
        keep = jnp.where((col_id >= at) & (col_id < at + PANEL), 0.0, out_ref[...])
        out_ref[...] = keep - update
        out_ref[at : at + PANEL, :] = rows


def spd_inverse(s, var):
    n = s.shape[0]
    return pl.pallas_call(
        inverse_kernel,
        out_shape=jax.ShapeDtypeStruct((n, n), jnp.float32),
        in_specs=[pl.BlockSpec(memory_space=pltpu.VMEM)] * 2,
        out_specs=pl.BlockSpec(memory_space=pltpu.VMEM),
        cost_estimate=pl.CostEstimate(flops=4 * n * n * n, bytes_accessed=8 * n * n, transcendentals=0),
        name="spd_inverse",
    )(s, var.reshape(1, n))


def footprint(start_ref, site_ref, cu_ref, cv_ref, su_ref, sv_ref, out_ref, coef_ref, site_col_ref):
    nobs = site_ref.shape[1]
    bands = cu_ref.shape[0]
    count = out_ref.shape[1] // MERIDIAN_TOTAL
    total = count + 2 * STEPS
    first = start_ref[0]
    chunk = 32
    lane = lax.broadcasted_iota(jnp.int32, (chunk, MERIDIAN_TOTAL), 1)
    site_col_ref[...] = jnp.broadcast_to(site_ref[...], (8, nobs)).T
    for t in range(total):
        band = first + (t - STEPS)
        inside = (band >= 0) & (band < bands)
        at = pl.ds(jnp.clip(band, 0, bands - 1), 1)
        cu = jnp.where(inside, cu_ref[at, :], 0.0)
        cv = jnp.where(inside, cv_ref[at, :], 0.0)
        west = jnp.where(su_ref[at, :] > 0, cu, 0.0)
        south = jnp.where(sv_ref[at, :] > 0, cv, 0.0)
        for k, line in enumerate((1.0 - cu - cv, west, cu - west, south, cv - south)):
            coef_ref[5 * t + k : 5 * t + k + 1, :] = line

    def coeff(t, k):
        return coef_ref[5 * t + k : 5 * t + k + 1, :]

    def body(i, carry):
        at = pl.multiple_of(i * chunk, chunk)
        site = site_col_ref[pl.ds(at, chunk), 0:1] - (first - STEPS) * MERIDIAN_TOTAL - lane
        v = [(site == t * MERIDIAN_TOTAL).astype(jnp.float32) for t in range(total)]
        for step in range(STEPS):
            low, high = (step + 1, total - step - 1)
            new = []
            for t in range(low, high):
                w = coeff(t, 0) * v[t]
                w = w + pltpu.roll(coeff(t, 1) * v[t], MERIDIAN_TOTAL - 1, 1)
                w = w + pltpu.roll(coeff(t, 2) * v[t], 1, 1)
                w = w + coeff(t + 1, 3) * v[t + 1]
                w = w + coeff(t - 1, 4) * v[t - 1]
                new.append(w)
            v = [None] * low + new + [None] * (total - high)
        for b in range(count):
            out_ref[pl.ds(at, chunk), b * MERIDIAN_TOTAL : (b + 1) * MERIDIAN_TOTAL] = v[STEPS + b]
        return carry

    lax.fori_loop(0, nobs // chunk, body, 0)


def rows_kernel(start_ref, site_ref, cu_ref, cv_ref, su_ref, sv_ref, cov_ref, rows_ref, near_ref, coef_ref, site_col_ref):
    footprint(start_ref, site_ref, cu_ref, cv_ref, su_ref, sv_ref, near_ref, coef_ref, site_col_ref)
    rows_ref[...] = jnp.dot(near_ref[...], cov_ref[...], precision=HIGHEST, preferred_element_type=jnp.float32)


def footprint_call(kernel, cells, nobs, width, scratch, operands):
    vmem = pl.BlockSpec(memory_space=pltpu.VMEM)
    total = cells // MERIDIAN_TOTAL + 2 * STEPS
    return pl.pallas_call(
        kernel,
        out_shape=jax.ShapeDtypeStruct((nobs, width), jnp.float32),
        in_specs=[pl.BlockSpec(memory_space=pltpu.SMEM)] + [vmem] * (len(operands) - 1),
        out_specs=vmem,
        scratch_shapes=[
            *scratch,
            pltpu.VMEM((5 * total + 6, MERIDIAN_TOTAL), jnp.float32),
            pltpu.VMEM((nobs, 8), jnp.int32),
        ],
        cost_estimate=pl.CostEstimate(flops=200 * 1000 * 1000, bytes_accessed=900000, transcendentals=0),
    )(*operands)


def gridded(site, winds):
    return [site.reshape(1, -1)] + [field.reshape(-1, MERIDIAN_TOTAL) for field in winds]


def observed_rows(covariance, band, site, *winds):
    rows_dev, cols_dev = covariance.shape
    assert rows_dev == MERIDIAN_TOTAL
    nobs = site.shape[0]
    operands = [band.reshape(1), *gridded(site, winds), covariance]
    near = [pltpu.VMEM((nobs, rows_dev), jnp.float32)]
    return footprint_call(rows_kernel, rows_dev, nobs, cols_dev, near, operands)


def column_footprint(cols_dev, band, site, *winds):
    operands = [band.reshape(1), *gridded(site, winds)]
    return footprint_call(footprint, cols_dev, site.shape[0], cols_dev, [], operands)


def everyone(chunk, axis):
    copies = jnp.broadcast_to(chunk, (lax.axis_size(axis), *chunk.shape))
    return lax.all_to_all(copies, axis, split_axis=0, concat_axis=0, tiled=True)


def scattered_sum(parts, axis):
    return jnp.sum(lax.all_to_all(parts, axis, split_axis=0, concat_axis=0, tiled=True), axis=0)


SWAP = [(0, 1), (1, 0)]


def halves(cells, dim, mine):
    width = cells.shape[dim] // 2
    low = lax.slice_in_dim(cells, 0, width, axis=dim)
    high = lax.slice_in_dim(cells, width, 2 * width, axis=dim)
    return jnp.where(mine == 0, low, high), jnp.where(mine == 0, high, low)


def joined(own, other, dim, mine):
    return jnp.concatenate(
        [jnp.where(mine == 0, own, other), jnp.where(mine == 0, other, own)], axis=dim
    )


def doubled(part, axis, reach):
    fellow = lax.ppermute(part, axis, [(i, i ^ reach) for i in range(lax.axis_size(axis))])
    return joined(part, fellow, 0, (lax.axis_index(axis) >> (reach.bit_length() - 1)) & 1)


def row_transported(cells, lon_speed, lat_speed, lon_sign, lat_sign, row_start):
    rows_dev, width = cells.shape
    row_bands = rows_dev // MERIDIAN_TOTAL

    def row_coeff(field):
        return lax.dynamic_slice_in_dim(field, row_start, rows_dev).reshape(
            row_bands, MERIDIAN_TOTAL, 1
        )

    row_cu, row_cv = (row_coeff(lon_speed), row_coeff(lat_speed))
    row_su, row_sv = (row_coeff(lon_sign), row_coeff(lat_sign))
    for _ in range(STEPS):
        padded = padded_2(cells, ((ROW, 0),), MERIDIAN_TOTAL)
        shaped = padded.reshape(row_bands + 2, MERIDIAN_TOTAL, width)
        cells = advect(
            shaped[1:-1], shaped[:-2], shaped[2:], row_cu, row_cv, row_su, row_sv, 0
        )
        cells = cells.reshape(rows_dev, width)
    return cells


def col_fields(lon_speed, lat_speed, lon_sign, lat_sign, col_start, cols_dev):
    margin = STEPS * MERIDIAN_TOTAL
    total_bands = cols_dev // MERIDIAN_TOTAL + 2 * STEPS

    def wide_coeff(field):
        extended = jnp.pad(field, (margin, margin))
        return lax.dynamic_slice_in_dim(extended, col_start, cols_dev + 2 * margin).reshape(
            1, total_bands, MERIDIAN_TOTAL
        )

    band_ids = col_start // MERIDIAN_TOTAL - STEPS + jnp.arange(total_bands, dtype=jnp.int32)
    inside = (
        ((band_ids >= 0) & (band_ids < PARALLEL_STRIPS))
        .astype(jnp.float32)
        .reshape(1, total_bands, 1)
    )
    return [wide_coeff(field) for field in (lon_speed, lat_speed, lon_sign, lat_sign)] + [inside]


def col_transported(padded, fields):
    rows, width = padded.shape
    current = padded.reshape(rows, width // MERIDIAN_TOTAL, MERIDIAN_TOTAL)
    for step in range(STEPS):
        count = current.shape[1]
        low, high = (step + 1, step + count - 1)
        cu, cv, su, sv, inside = (field[:, low:high] for field in fields)
        current = (
            advect(current[:, 1:-1], current[:, :-2], current[:, 2:], cu, cv, su, sv, 1) * inside
        )
    return current.reshape(rows, -1)


def shards(
    covariance, lon_speed, lat_speed, lon_sign, lat_sign, measurement_site_position, obs_var
):
    rows_dev, cols_dev = covariance.shape
    nobs = measurement_site_position.shape[0]
    lat_half, core = lax.axis_index("yl"), lax.axis_index("co")
    row, col = lax.axis_index(ROW), lax.axis_index(COL)
    row_start, col_start = row * rows_dev, col * cols_dev
    margin = STEPS * MERIDIAN_TOTAL
    dot = functools.partial(
        lax.dot_general, precision=HIGHEST, preferred_element_type=jnp.float32
    )
    winds = (lon_speed, lat_speed, lon_sign, lat_sign)
    hp = observed_rows(
        covariance, row_start // MERIDIAN_TOTAL, measurement_site_position, *winds
    )
    spread = column_footprint(
        cols_dev, col_start // MERIDIAN_TOTAL, measurement_site_position, *winds
    )

    own, other = halves(hp, 0, core)
    fellow = lax.ppermute(other, "co", SWAP)
    own, other = halves(own + fellow, 0, lat_half)
    fellow = lax.ppermute(other, "yl", SWAP)
    hp = own + fellow
    deep = lax.axis_size("z")
    hp = scattered_sum(hp.reshape(deep, nobs // 4 // deep, cols_dev), "z")

    forecast = row_transported(covariance, *winds, row_start)
    pht = dot(spread, forecast, (((1,), (1,)), ((), ())))
    fields = col_fields(*winds, col_start, cols_dev)

    sides = lax.axis_size(COL)
    hpht = dot(hp, spread, (((1,), (1,)), ((), ())))
    mine = jnp.concatenate([hp, hpht], axis=1)
    pht = pht.reshape(sides, nobs // sides, rows_dev)
    packed = jnp.broadcast_to(mine.reshape(1, -1, rows_dev), (sides, mine.size // rows_dev, rows_dev))
    packed = lax.all_to_all(
        jnp.concatenate([packed, pht], axis=1), COL, split_axis=0, concat_axis=0, tiled=True
    )
    packed, forecast = lax.optimization_barrier((packed, forecast))
    found = packed[:, : mine.size // rows_dev].reshape(sides, *mine.shape)
    pht = jnp.sum(packed[:, mine.size // rows_dev :], axis=0)
    hpht = jnp.sum(found[:, :, cols_dev:], axis=0)
    near = lax.dynamic_slice_in_dim(
        jnp.pad(found[:, :, :cols_dev], ((1, 1), (0, 0), (0, 0))), col, 3
    )
    hp = jnp.concatenate([near[0, :, cols_dev - margin :], near[1], near[2, :, :margin]], axis=1)
    hp = col_transported(hp, fields)

    block = jnp.concatenate([hp, hpht], axis=1)
    block = everyone(block, "z").reshape(nobs // 4, cols_dev + nobs)
    forecast = padded_2(forecast, ((COL, 1),), margin)
    forecast = col_transported(forecast, fields)
    fellow = lax.ppermute(block, "yl", SWAP)
    block = joined(block, fellow, 0, lat_half)
    fellow = lax.ppermute(block, "co", SWAP)
    block = joined(block, fellow, 0, core)
    hp, hpht = block[:, :cols_dev], block[:, cols_dev:]

    for axis, reach in (("x", 1), ("x", 2), ("yh", 1), ("yh", 2)):
        pht = doubled(pht, axis, reach)
    inverse = spd_inverse(hpht, obs_var)
    gain = dot(inverse, pht, (((1,), (0,)), ((), ())))
    return forecast - dot(gain, hp, (((0,), (0,)), ((), ())))


def solution(mesh):
    fine = Mesh(mesh.devices.reshape(2, 16, 2, 4, 4), ROW + COL)
    return jax.shard_map(
        shards,
        mesh=fine,
        in_specs=(P(ROW, COL), P(), P(), P(), P(), P(), P()),
        out_specs=P(ROW, COL),
        check_vma=False,
    )
```
